32 devices in a mesh: groups: 2 (over y), tm: 4 (over z), dp: 2 (over x), width: 2 (over core).
Axes of the slice: x: 2, y: 2, z: 4, core: 2. Of those that a mesh axis runs over, the one named last changes fastest.
Arguments:
- clips: bfloat16 [4, 16, 8, 64, 128], P(('groups', 'dp'), 'tm', 'width'), parts along dimension 0, may hold values from -16.5 to 16.5
- gain: float32 [128], replicated, may hold values from 0.5 to 1.5
- bias: float32 [128], replicated, may hold values from -3 to 3
- weight: bfloat16 [3456, 256], replicated, may hold values from -0.109375 to 0.109375
- cotangent: bfloat16 [4, 16, 8, 64, 256], P(('groups', 'dp'), 'tm', 'width'), parts along dimension 0, may hold values from -6 to 6
Outputs:
- output: bfloat16 [4, 16, 8, 64, 256], P(('groups', 'dp'), 'tm', 'width'), parts along dimension 0
- grad_weight: float32 [6912, 256], P(('groups', 'tm', 'dp'), 'width'), parts along dimension 0
- grad_gain: float32 [256], P('groups'), parts along dimension 0
- grad_bias: float32 [256], P('groups'), parts along dimension 0
The draws below stay inside these ranges and needn't reach their ends.
There are 2 independent parts, one for each index of `groups`. The reference program is written for one: setup_inputs(seed, part) draws one part's arguments, and reference() takes and returns one part's arrays. A program takes and returns all parts, laid end to end along the dimension named above; an argument that names none is the same for every part. Nothing has to cross between parts.
All inputs are finite; a program needn't handle non-finite values.
Results may differ from the reference program's by a relative error of at most 0.0049.
Values may be sent and summed in bfloat16 or wider, within the bound.
No kernel may reach another device: no remote copies, remote signals or barrier semaphores. Data moves between devices by JAX's collectives and lax.ppermute only.
A program may use at most 64 MiB of HBM per device.

```python
import math
import jax
import jax.numpy as jnp
from jax import lax

CI = 128
CO = 256
GROUPS = 32
ROWS = 4
COLS = 64
CLIPS = 2
FRAMES = 16
HEIGHT = 8


def draw_clips(key, part):
    key_mean = jax.random.fold_in(key, 11)
    key_noise = jax.random.fold_in(key, 12)
    key_drift = jax.random.fold_in(key, 13)
    key_wave = jax.random.fold_in(key, 14)
    key_phase = jax.random.fold_in(key, 15)
    key_jitter = jax.random.fold_in(key, 16)
    halves = HEIGHT // ROWS
    frame_pos = jnp.arange(FRAMES, dtype=jnp.float32)
    trend = 1.0 + 2.0 * frame_pos / float(max(FRAMES - 1, 1))
    log_span = math.log(max(FRAMES / 8.0, 1.0))
    period = float(FRAMES) * jnp.exp(-jax.random.uniform(key_wave, (CLIPS, 1, halves), jnp.float32, 0.0, 1.0) * log_span)
    phase = jax.random.uniform(key_phase, (CLIPS, 1, halves), jnp.float32, -jnp.pi, jnp.pi)
    jitter = jax.random.uniform(key_jitter, (CLIPS, FRAMES, halves), jnp.float32, -1.0, 1.0)
    factor = 0.75 + 0.15 * jnp.sin(2.0 * jnp.pi * frame_pos[None, :, None] / period + phase) + 0.1 * jitter
    growth = trend[None, :, None] * factor
    row_half = jnp.arange(HEIGHT, dtype=jnp.int32) // ROWS
    growth_rows = growth[:, :, row_half]
    base_mean = 0.5 * jax.random.normal(key_mean, (CI,), jnp.float32)
    drift = 0.4 * jax.random.normal(key_drift, (CLIPS, FRAMES, 1, 1, CI), jnp.float32)
    channel_mean = jnp.clip(base_mean + drift, -1.5, 1.5)
    noise = jnp.clip(jax.random.normal(key_noise, (CLIPS, FRAMES, HEIGHT, COLS, CI), jnp.float32), -4.0, 4.0)
    return ((channel_mean + noise) * growth_rows[:, :, :, None, None]).astype(jnp.bfloat16)


def level_of(rng, dims, pieces, smallest, high):
    factor_of, own = 1.0, jax.random.fold_in(rng, 6)
    for position, blocks in pieces:
        steps = jnp.exp(jax.random.uniform(jax.random.fold_in(own, position), (blocks,), jnp.float32, smallest / len(pieces), high / len(pieces)))
        factor_of = factor_of * jnp.repeat(steps, dims[position] // blocks).reshape([-1 if axis == position else 1 for axis in range(len(dims))])
    return factor_of


def normal_values(rng, shape, width, bound, cuts=(), kind=jnp.bfloat16):
    loudness = level_of(rng, shape, cuts, -0.22, 0.18) if cuts else 1.0
    entries = jax.random.normal(rng, shape, jnp.float32) * width * loudness
    return jnp.minimum(jnp.maximum(entries, -bound), bound).astype(kind)


def setup_inputs(seed: int = 0, part: int = 0) -> dict:
    key_list = jax.random.split(jax.random.key(seed), 6)
    own_keys = jax.random.split(jax.random.fold_in(key_list[5], part), 6)
    clips = draw_clips(jax.random.fold_in(jax.random.fold_in(key_list[5], part), 71), part)
    gain = jnp.clip(jax.random.uniform(key_list[1], (CI,), jnp.float32, 0.5, 1.5), 0.5, 1.5)
    bias = normal_values(key_list[2], (CI,), 0.5, 3.0, (), jnp.float32)
    weight = normal_values(key_list[3], (27 * CI, CO), (27 * CI) ** -0.5, 0.109375)
    cotangent = normal_values(own_keys[4], (CLIPS, FRAMES, HEIGHT, COLS, CO), 1.0, 6.0, ((0, 2), (1, 4), (2, 2)))
    return dict(clips=clips, gain=gain, bias=bias, weight=weight, cotangent=cotangent)


def convolve(hidden_in, kernel):
    result = lax.conv_general_dilated(hidden_in[None], kernel, (1, 1, 1), ((2, 0), (1, 1), (1, 1)), dimension_numbers=('NDHWC', 'DHWIO', 'NDHWC'), precision=lax.Precision.HIGHEST)
    return result[0]

def reference(clips, gain, bias, weight, cotangent):
    kernel = weight.astype(jnp.float32).reshape(3, 3, 3, CI, CO)
    per_group = CI // GROUPS

    def one_clip(pair):
        frames_in, cot_clip = pair
        values = frames_in.astype(jnp.float32)
        grouped = values.reshape(FRAMES, HEIGHT, COLS, GROUPS, per_group)
        first_sum = jnp.cumsum(lax.optimization_barrier(jnp.sum(grouped, axis=(1, 2, 4))), axis=0)
        square_sum = jnp.cumsum(lax.optimization_barrier(jnp.sum(grouped * grouped, axis=(1, 2, 4))), axis=0)
        count = (jnp.arange(FRAMES, dtype=jnp.float32) + 1.0) * float(HEIGHT * COLS * per_group)
        mean = first_sum / count[:, None]
        variance = square_sum / count[:, None] - mean * mean
        inverse = lax.rsqrt(variance + 1e-05)
        normed = ((grouped - mean[:, None, None, :, None]) * inverse[:, None, None, :, None]).reshape(FRAMES, HEIGHT, COLS, CI)
        act = normed * gain + bias
        sigma = jax.nn.sigmoid(act)
        hidden = (act * sigma).astype(jnp.bfloat16)
        result, back = jax.vjp(convolve, hidden.astype(jnp.float32), kernel)
        grad_hidden, grad_kernel = back(cot_clip.astype(jnp.float32))
        grad_act = grad_hidden * sigma * (1.0 + act * (1.0 - sigma))
        return (result.astype(jnp.bfloat16), grad_kernel.reshape(27 * CI, CO), lax.optimization_barrier(jnp.sum(grad_act * normed, axis=(0, 1, 2))), lax.optimization_barrier(jnp.sum(grad_act, axis=(0, 1, 2))))
    output, grad_kernels, gains, biases = lax.map(one_clip, (clips, cotangent))
    return (output, lax.optimization_barrier(jnp.sum(grad_kernels, axis=0)), lax.optimization_barrier(jnp.sum(gains, axis=0)), lax.optimization_barrier(jnp.sum(biases, axis=0)))
```

```python
import functools

import jax
import jax.numpy as jnp
from jax import lax
from jax.experimental import pallas as pl
from jax.experimental.pallas import tpu as pltpu
from jax.sharding import PartitionSpec as P

GROUPS = 32
F32, BF16 = jnp.float32, jnp.bfloat16
VMEM = pl.BlockSpec(memory_space=pltpu.VMEM)
SMEM = pl.BlockSpec(memory_space=pltpu.SMEM)


def call(kernel, out_shape, inputs, scratch=(), flops=0, scalars=0, trans=0):
    outs = jax.tree.leaves(out_shape)
    moved = sum(v.size * v.dtype.itemsize for v in list(inputs) + list(outs))
    return pl.pallas_call(
        kernel,
        out_shape=out_shape,
        in_specs=[SMEM] * scalars + [VMEM] * (len(inputs) - scalars),
        out_specs=jax.tree.map(lambda _: VMEM, out_shape),
        scratch_shapes=list(scratch),
        cost_estimate=pl.CostEstimate(flops=flops, bytes_accessed=moved, transcendentals=trans),
        compiler_params=pltpu.CompilerParams(vmem_limit_bytes=40 << 20),
    )(*inputs)


def group_sum(rows, per_group):
    lane = lax.broadcasted_iota(jnp.int32, rows.shape, 1)
    lanes = rows.shape[1]
    step = 1
    while step < per_group:
        up = pltpu.roll(rows, lanes - step, 1)
        down = pltpu.roll(rows, step, 1)
        rows = rows + jnp.where((lane // step) % 2 == 0, up, down)
        step *= 2
    return rows


def sums_kernel(per_group, x_ref, o_ref):
    frames = x_ref.shape[0]
    firsts, squares = [], []
    for t in range(frames):
        v = x_ref[t].astype(F32)
        firsts.append(jnp.sum(v, axis=0, keepdims=True))
        squares.append(jnp.sum(v * v, axis=0, keepdims=True))
    o_ref[...] = group_sum(jnp.concatenate(firsts + squares, axis=0), per_group)


def frame_stats(place, stats_ref, frames, per_frame):
    devices = stats_ref.shape[0]
    mine = place[0]
    own = stats_ref[0]
    before = jnp.zeros_like(own)
    behind = jnp.zeros_like(own)
    for x in range(1, devices):
        other = jnp.bitwise_xor(mine, x)
        rows = stats_ref[x]
        before = before + jnp.where(other < mine - 1, rows, 0.0)
        behind = behind + jnp.where(other == mine - 1, rows, 0.0)

    def total(rows, at):
        return jnp.sum(rows[at : at + frames], axis=0, keepdims=True)

    first, square = total(before, 0), total(before, frames)
    means, inverses = [], []
    for k in range(2 * frames):
        rows, t = (behind, k) if k < frames else (own, k - frames)
        first = first + rows[t : t + 1]
        square = square + rows[frames + t : frames + t + 1]
        if k < frames - 2:
            continue
        shown = jnp.maximum(mine * frames + k - frames + 1, 1).astype(F32) * per_frame
        mean = first / shown
        variance = square / shown - mean * mean
        means.append(mean)
        inverses.append(lax.rsqrt(variance + 1e-05))
    return means, inverses


def grad_hidden_kernel(place, g_ref, next_ref, edge_ref, w_ref, gp_ref, o_ref, z_ref):
    frames, rows, cols, chan_out = g_ref.shape
    chan_in = o_ref.shape[1]
    core = place[1]
    edge = edge_ref[...]
    zero = jnp.zeros_like(edge)
    gp_ref[:, 0] = jnp.where(core == 0, zero, edge)
    gp_ref[:, rows + 1] = jnp.where(core == 0, edge, zero)
    gp_ref[:frames, 1 : rows + 1] = g_ref[...]
    gp_ref[frames:, 1 : rows + 1] = next_ref[...]
    cells = frames * rows * cols
    for a in range(3):
        for b in range(3):
            tap = a * 3 + b
            window = gp_ref[2 - a : 2 - a + frames, 2 - b : 2 - b + rows].reshape(cells, chan_out)
            part = lax.dot_general(
                window,
                w_ref[tap * 3 * chan_in : (tap + 1) * 3 * chan_in],
                (((1,), (1,)), ((), ())),
                preferred_element_type=F32,
            )
            if tap == 0:
                z_ref[...] = part
            else:
                z_ref[...] += part
    col = lax.broadcasted_iota(jnp.int32, (cells, chan_in), 0) % cols
    left = jnp.where(col == cols - 1, 0.0, pltpu.roll(z_ref[:, :chan_in], cells - 1, 0))
    right = jnp.where(col == 0, 0.0, pltpu.roll(z_ref[:, 2 * chan_in :], 1, 0))
    o_ref[...] = left + z_ref[:, chan_in : 2 * chan_in] + right


def kernel_grad_kernel(per_frame, place, stats_ref, gain_ref, bias_ref, x_ref, gp_ref, keep_ref, send_ref, ht_ref):
    frames, cells, chan_in = x_ref.shape
    rows = gp_ref.shape[1] - 2
    cols = gp_ref.shape[2]
    chan_out = gp_ref.shape[3]
    core = place[1]
    means, inverses = frame_stats(place, stats_ref, frames, per_frame)
    gain, bias = gain_ref[...], bias_ref[...]
    block = 2 * cols
    lane = lax.broadcasted_iota(jnp.int32, (chan_in, block), 1) % cols
    for t in range(frames):
        for half in range(cells // block):
            v = x_ref[t, half * block : (half + 1) * block].astype(F32)
            act = (v - means[2 + t]) * inverses[2 + t] * gain + bias
            hidden = (act * lax.logistic(act)).astype(BF16).astype(F32)
            turned = hidden.T
            at = t * cells + half * block
            earlier = jnp.where(lane == 0, 0.0, pltpu.roll(turned, 1, 1))
            later = jnp.where(lane == cols - 1, 0.0, pltpu.roll(turned, block - 1, 1))
            ht_ref[:chan_in, at : at + block] = earlier.astype(BF16)
            ht_ref[chan_in : 2 * chan_in, at : at + block] = turned.astype(BF16)
            ht_ref[2 * chan_in :, at : at + block] = later.astype(BF16)
    mine = chan_out // 2
    for a in range(3):
        for b in range(3):
            tap = a * 3 + b
            window = gp_ref[2 - a : 2 - a + frames, 2 - b : 2 - b + rows].reshape(frames * cells, chan_out)
            part = jnp.dot(ht_ref[...], window, preferred_element_type=F32)
            at = tap * 3 * chan_in
            low, high = part[:, :mine], part[:, mine:]
            keep_ref[at : at + 3 * chan_in] = jnp.where(core == 0, low, high)
            send_ref[at : at + 3 * chan_in] = jnp.where(core == 0, high, low).astype(BF16)


def gain_kernel(per_frame, place, stats_ref, gain_ref, bias_ref, x_ref, gh_ref, o_ref):
    frames, cells, chan_in = x_ref.shape
    means, inverses = frame_stats(place, stats_ref, frames, per_frame)
    gain, bias = gain_ref[...], bias_ref[...]
    by_gain = jnp.zeros((1, chan_in), F32)
    by_bias = jnp.zeros((1, chan_in), F32)
    for t in range(frames):
        normed = (x_ref[t].astype(F32) - means[2 + t]) * inverses[2 + t]
        act = normed * gain + bias
        sigma = lax.logistic(act)
        grad_act = gh_ref[t * cells : (t + 1) * cells] * sigma * (1.0 + act * (1.0 - sigma))
        by_gain = by_gain + jnp.sum(grad_act * normed, axis=0, keepdims=True)
        by_bias = by_bias + jnp.sum(grad_act, axis=0, keepdims=True)
    o_ref[...] = jnp.concatenate([by_gain, by_bias], axis=0)


def output_kernel(
    per_frame, place, stats_ref, gain_ref, bias_ref, x_ref, prev_ref, edge_ref, w_ref, o_ref, h_ref, acc_ref
):
    frames, rows, cols, chan_in = x_ref.shape
    chan_out = o_ref.shape[1]
    mine, core = place[0], place[1]
    means, inverses = frame_stats(place, stats_ref, frames, per_frame)
    gain, bias = gain_ref[...], bias_ref[...]

    def put(f, r0, count, value, keep):
        act = (value.astype(F32) - means[f]) * inverses[f] * gain + bias
        hidden = act * lax.logistic(act)
        if keep is not None:
            hidden = jnp.where(keep, hidden, 0.0)
        n = count * cols
        col = lax.broadcasted_iota(jnp.int32, (n, chan_in), 0) % cols
        earlier = jnp.where(col == 0, 0.0, pltpu.roll(hidden, 1, 0))
        later = jnp.where(col == cols - 1, 0.0, pltpu.roll(hidden, n - 1, 0))
        for d, piece in enumerate((earlier, hidden, later)):
            h_ref[f, r0 : r0 + count, :, d * chan_in : (d + 1) * chan_in] = piece.astype(BF16).reshape(
                count, cols, chan_in
            )

    for f in range(frames + 2):
        inside = (mine > 0) if f < 2 else None
        value = prev_ref[f] if f < 2 else x_ref[f - 2]
        put(f, 1, rows, value.reshape(rows * cols, chan_in), inside)
        for r0, here in ((0, core == 1), (rows + 1, core == 0)):
            put(f, r0, 1, edge_ref[f], here if inside is None else jnp.logical_and(here, inside))
    cells = frames * rows * cols
    for a in range(3):
        for b in range(3):
            tap = a * 3 + b
            window = h_ref[a : a + frames, b : b + rows].reshape(cells, 3 * chan_in)
            part = jnp.dot(window, w_ref[tap * 3 * chan_in : (tap + 1) * 3 * chan_in], preferred_element_type=F32)
            if tap == 0:
                acc_ref[...] = part
            elif tap < 8:
                acc_ref[...] += part
            else:
                o_ref[...] = (acc_ref[...] + part).astype(BF16)


def bits_of(axis):
    return [1 << k for k in range((lax.axis_size(axis) - 1).bit_length())]


def swap(value, axis, step):
    return lax.ppermute(value, axis, [(i, i ^ step) for i in range(lax.axis_size(axis))])


def gather_xor(value, axis):
    value = value[None]
    for step in bits_of(axis):
        value = jnp.concatenate([value, swap(value, axis, step)], axis=0)
    return value


def all_sum(value, axes):
    for axis in axes:
        for step in bits_of(axis):
            value = value + swap(value, axis, step)
    return value


def halve(value, axis, dims):
    value = jnp.moveaxis(value, dims, 0) if dims else value
    rest = value.shape[1:]
    me = lax.axis_index(axis)
    for step in bits_of(axis):
        value = value.reshape((value.shape[0] // 2, 2) + rest)
        bit = (me // step) % 2
        keep = lax.dynamic_index_in_dim(value, bit, 1, keepdims=False)
        send = lax.dynamic_index_in_dim(value, 1 - bit, 1, keepdims=False)
        value = keep + swap(send.astype(BF16), axis, step).astype(F32)
    return value[0]


def body(clips, gain, bias, weight, cotangent):
    x, g = clips[0], cotangent[0]
    frames, rows, cols, chan_in = x.shape
    chan_out = g.shape[-1]
    per_group = chan_in // GROUPS
    tm, dp, width = (lax.axis_size(name) for name in ("tm", "dp", "width"))
    per_frame = float(rows * width * cols * per_group)
    z, core = lax.axis_index("tm"), lax.axis_index("width")
    place = jnp.stack([z, core]).astype(jnp.int32)
    cells = rows * cols
    shape = jax.ShapeDtypeStruct
    flat = x.reshape(frames, cells, chan_in)
    conv_flops = 2 * frames * cells * 27 * chan_in * chan_out

    sums = call(functools.partial(sums_kernel, per_group), shape((2 * frames, chan_in), F32), [flat])
    sums = sums + swap(sums, "width", 1)
    stats = gather_xor(sums, "tm")

    up = [(i, i + 1) for i in range(tm - 1)]
    down = [(i + 1, i) for i in range(tm - 1)]
    g_next = lax.ppermute(g[:2], "tm", down)
    x_prev = lax.ppermute(x[frames - 2 :], "tm", up)

    def edge_row(value):
        return jnp.where(core == 0, value[:, rows - 1], value[:, 0])

    g_edge = swap(jnp.concatenate([edge_row(g), edge_row(g_next)], axis=0), "width", 1)
    x_edge = swap(jnp.concatenate([edge_row(x_prev), edge_row(x)], axis=0), "width", 1)

    gp, grad_hidden = call(
        grad_hidden_kernel,
        (shape((frames + 2, rows + 2, cols, chan_out), BF16), shape((frames * cells, chan_in), F32)),
        [place, g, g_next, g_edge, weight],
        [pltpu.VMEM((frames * cells, 3 * chan_in), F32)],
        conv_flops,
        1,
    )
    gain_row, bias_row = gain[None], bias[None]
    norm = [place, stats, gain_row, bias_row]
    keep, send = call(
        functools.partial(kernel_grad_kernel, per_frame),
        (shape((27 * chan_in, chan_out // 2), F32), shape((27 * chan_in, chan_out // 2), BF16)),
        norm + [flat, gp],
        [pltpu.VMEM((3 * chan_in, frames * cells), BF16)],
        conv_flops,
        1,
    )
    total = keep + swap(send, "width", 1).astype(F32)
    local = call(
        functools.partial(gain_kernel, per_frame),
        shape((2, chan_in), F32),
        norm + [flat, grad_hidden],
        scalars=1,
    )
    output = call(
        functools.partial(output_kernel, per_frame),
        shape((frames * cells, chan_out), BF16),
        norm + [x, x_prev, x_edge, weight],
        [
            pltpu.VMEM((frames + 2, rows + 2, cols, 3 * chan_in), BF16),
            pltpu.VMEM((frames * cells, chan_out), F32),
        ],
        conv_flops,
        1,
    )
    share = 27 * chan_in // (tm * dp)
    cut = max(share * 11 // 16 // 16 * 16, 1)
    total = total.reshape(tm, dp, share, chan_out // 2)
    one = halve(halve(total[:, :, :cut], "dp", 1), "tm", 0)
    two = halve(halve(total[:, :, cut:], "tm", 0), "dp", 0)
    grad_weight = jnp.concatenate([one, two], axis=0)
    grads = all_sum(local, ("width", "dp", "tm"))
    return (output.reshape(1, frames, rows, cols, chan_out), grad_weight, grads[0], grads[1])


def solution(mesh):
    return jax.shard_map(
        body,
        mesh=mesh,
        in_specs=(
            P(("groups", "dp"), "tm", "width", None, None),
            P(),
            P(),
            P(),
            P(("groups", "dp"), "tm", "width", None, None),
        ),
        out_specs=(
            P(("groups", "dp"), "tm", "width", None, None),
            P(("groups", "tm", "dp"), "width"),
            P("groups"),
            P("groups"),
        ),
        check_vma=False,
    )
```

```python
import functools

import jax
import jax.numpy as jnp
from jax import lax
from jax.experimental import pallas as pl
from jax.experimental.pallas import tpu as pltpu
from jax.sharding import PartitionSpec as P

GROUPS = 32
F32, BF16 = jnp.float32, jnp.bfloat16
VMEM = pl.BlockSpec(memory_space=pltpu.VMEM)
SMEM = pl.BlockSpec(memory_space=pltpu.SMEM)
ANY = pl.BlockSpec(memory_space=pl.ANY)


def call(kernel, out_shape, inputs, scratch=(), flops=0, scalars=0, far=0):
    outs = jax.tree.leaves(out_shape)
    moved = sum(v.size * v.dtype.itemsize for v in list(inputs) + list(outs))
    return pl.pallas_call(
        kernel,
        out_shape=out_shape,
        in_specs=[SMEM] * scalars + [VMEM] * (len(inputs) - scalars - far) + [ANY] * far,
        out_specs=jax.tree.map(lambda _: VMEM, out_shape),
        scratch_shapes=list(scratch),
        cost_estimate=pl.CostEstimate(flops=flops, bytes_accessed=moved, transcendentals=0),
        compiler_params=pltpu.CompilerParams(vmem_limit_bytes=16 << 20),
    )(*inputs)


def group_sum(rows, per_group):
    lane = lax.broadcasted_iota(jnp.int32, rows.shape, 1)
    lanes = rows.shape[1]
    step = 1
    while step < per_group:
        up = pltpu.roll(rows, lanes - step, 1)
        down = pltpu.roll(rows, step, 1)
        rows = rows + jnp.where((lane // step) % 2 == 0, up, down)
        step *= 2
    return rows


def sums_kernel(per_group, x_ref, o_ref):
    frames = x_ref.shape[0]
    firsts, squares = [], []
    for t in range(frames):
        v = x_ref[t].astype(F32)
        firsts.append(jnp.sum(v, axis=0, keepdims=True))
        squares.append(jnp.sum(v * v, axis=0, keepdims=True))
    o_ref[...] = group_sum(jnp.concatenate(firsts + squares, axis=0), per_group)


def frame_stats(place, stats_ref, frames, per_frame):
    devices = stats_ref.shape[0]
    mine = place[0]
    own = stats_ref[0]
    before = jnp.zeros_like(own)
    behind = jnp.zeros_like(own)
    for x in range(1, devices):
        other = jnp.bitwise_xor(mine, x)
        rows = stats_ref[x]
        before = before + jnp.where(other < mine - 1, rows, 0.0)
        behind = behind + jnp.where(other == mine - 1, rows, 0.0)

    def total(rows, at):
        return jnp.sum(rows[at : at + frames], axis=0, keepdims=True)

    first, square = total(before, 0), total(before, frames)
    means, inverses = [], []
    for k in range(2 * frames):
        rows, t = (behind, k) if k < frames else (own, k - frames)
        first = first + rows[t : t + 1]
        square = square + rows[frames + t : frames + t + 1]
        if k < frames - 2:
            continue
        shown = jnp.maximum(mine * frames + k - frames + 1, 1).astype(F32) * per_frame
        mean = first / shown
        variance = square / shown - mean * mean
        means.append(mean)
        inverses.append(lax.rsqrt(variance + 1e-05))
    return means, inverses


def pad_cotangent(core, g_ref, next_ref, edge_ref, gp_ref):
    frames, rows = g_ref.shape[:2]
    edge = edge_ref[...]
    zero = jnp.zeros_like(edge)
    gp_ref[:, 0] = jnp.where(core == 0, zero, edge)
    gp_ref[:, rows + 1] = jnp.where(core == 0, edge, zero)
    gp_ref[:frames, 1 : rows + 1] = g_ref[...]
    gp_ref[frames:, 1 : rows + 1] = next_ref[...]


def tap_copies(w_hbm, w_ref, sems):
    each = w_hbm.shape[0] // 9
    return [
        pltpu.make_async_copy(w_hbm.at[pl.ds(k * each, each)], w_ref.at[pl.ds(k * each, each)], sems.at[k])
        for k in range(9)
    ]


def grad_hidden_kernel(place, g_ref, next_ref, edge_ref, w_hbm, o_ref, gp_ref, z_ref, w_ref, sems):
    frames, rows, cols, chan_out = g_ref.shape
    chan_in = o_ref.shape[1]
    copies = tap_copies(w_hbm, w_ref, sems)
    for copy in copies:
        copy.start()
    pad_cotangent(place[1], g_ref, next_ref, edge_ref, gp_ref)
    cells = frames * rows * cols
    for a in range(3):
        for b in range(3):
            tap = a * 3 + b
            window = gp_ref[2 - a : 2 - a + frames, 2 - b : 2 - b + rows].reshape(cells, chan_out)
            copies[tap].wait()
            part = lax.dot_general(
                window,
                w_ref[tap * 3 * chan_in : (tap + 1) * 3 * chan_in],
                (((1,), (1,)), ((), ())),
                preferred_element_type=F32,
            )
            if tap == 0:
                z_ref[...] = part
            else:
                z_ref[...] += part
    col = lax.broadcasted_iota(jnp.int32, (cells, chan_in), 0) % cols
    left = jnp.where(col == cols - 1, 0.0, pltpu.roll(z_ref[:, :chan_in], cells - 1, 0))
    right = jnp.where(col == 0, 0.0, pltpu.roll(z_ref[:, 2 * chan_in :], 1, 0))
    o_ref[...] = left + z_ref[:, chan_in : 2 * chan_in] + right


def kernel_grad_kernel(per_frame, place, stats_ref, gain_ref, bias_ref, x_ref, g_ref, next_ref, edge_ref, keep_ref, send_ref, gp_ref, ht_ref):
    frames, cells, chan_in = x_ref.shape
    rows, cols, chan_out = g_ref.shape[1:]
    core = place[1]
    pad_cotangent(core, g_ref, next_ref, edge_ref, gp_ref)
    means, inverses = frame_stats(place, stats_ref, frames, per_frame)
    gain, bias = gain_ref[...], bias_ref[...]
    block = 2 * cols
    lane = lax.broadcasted_iota(jnp.int32, (chan_in, block), 1) % cols
    for t in range(frames):
        for half in range(cells // block):
            v = x_ref[t, half * block : (half + 1) * block].astype(F32)
            act = (v - means[2 + t]) * inverses[2 + t] * gain + bias
            hidden = (act * lax.logistic(act)).astype(BF16).astype(F32)
            turned = hidden.T
            at = t * cells + half * block
            earlier = jnp.where(lane == 0, 0.0, pltpu.roll(turned, 1, 1))
            later = jnp.where(lane == cols - 1, 0.0, pltpu.roll(turned, block - 1, 1))
            ht_ref[:chan_in, at : at + block] = earlier.astype(BF16)
            ht_ref[chan_in : 2 * chan_in, at : at + block] = turned.astype(BF16)
            ht_ref[2 * chan_in :, at : at + block] = later.astype(BF16)
    mine = chan_out // 2
    for a in range(3):
        for b in range(3):
            tap = a * 3 + b
            window = gp_ref[2 - a : 2 - a + frames, 2 - b : 2 - b + rows].reshape(frames * cells, chan_out)
            part = jnp.dot(ht_ref[...], window, preferred_element_type=F32)
            at = tap * 3 * chan_in
            low, high = part[:, :mine], part[:, mine:]
            keep_ref[at : at + 3 * chan_in] = jnp.where(core == 0, low, high)
            send_ref[at : at + 3 * chan_in] = jnp.where(core == 0, high, low).astype(BF16)


def gain_kernel(per_frame, place, stats_ref, gain_ref, bias_ref, x_ref, gh_ref, o_ref):
    frames, cells, chan_in = x_ref.shape
    means, inverses = frame_stats(place, stats_ref, frames, per_frame)
    gain, bias = gain_ref[...], bias_ref[...]
    by_gain = jnp.zeros((1, chan_in), F32)
    by_bias = jnp.zeros((1, chan_in), F32)
    for t in range(frames):
        normed = (x_ref[t].astype(F32) - means[2 + t]) * inverses[2 + t]
        act = normed * gain + bias
        sigma = lax.logistic(act)
        grad_act = gh_ref[t * cells : (t + 1) * cells] * sigma * (1.0 + act * (1.0 - sigma))
        by_gain = by_gain + jnp.sum(grad_act * normed, axis=0, keepdims=True)
        by_bias = by_bias + jnp.sum(grad_act, axis=0, keepdims=True)
    o_ref[...] = jnp.concatenate([by_gain, by_bias], axis=0)


def output_kernel(
    per_frame, place, stats_ref, gain_ref, bias_ref, x_ref, prev_ref, edge_ref, w_hbm, o_ref, h_ref, acc_ref, w_ref, sems
):
    frames, rows, cols, chan_in = x_ref.shape
    chan_out = o_ref.shape[1]
    copies = tap_copies(w_hbm, w_ref, sems)
    for copy in copies:
        copy.start()
    mine, core = place[0], place[1]
    means, inverses = frame_stats(place, stats_ref, frames, per_frame)
    gain, bias = gain_ref[...], bias_ref[...]

    def put(f, r0, count, value, keep):
        act = (value.astype(F32) - means[f]) * inverses[f] * gain + bias
        hidden = act * lax.logistic(act)
        if keep is not None:
            hidden = jnp.where(keep, hidden, 0.0)
        n = count * cols
        col = lax.broadcasted_iota(jnp.int32, (n, chan_in), 0) % cols
        earlier = jnp.where(col == 0, 0.0, pltpu.roll(hidden, 1, 0))
        later = jnp.where(col == cols - 1, 0.0, pltpu.roll(hidden, n - 1, 0))
        for d, piece in enumerate((earlier, hidden, later)):
            h_ref[f, r0 : r0 + count, :, d * chan_in : (d + 1) * chan_in] = piece.astype(BF16).reshape(
                count, cols, chan_in
            )

    for f in range(frames + 2):
        inside = (mine > 0) if f < 2 else None
        value = prev_ref[f] if f < 2 else x_ref[f - 2]
        put(f, 1, rows, value.reshape(rows * cols, chan_in), inside)
        for r0, here in ((0, core == 1), (rows + 1, core == 0)):
            put(f, r0, 1, edge_ref[f], here if inside is None else jnp.logical_and(here, inside))
    cells = frames * rows * cols
    for a in range(3):
        for b in range(3):
            tap = a * 3 + b
            window = h_ref[a : a + frames, b : b + rows].reshape(cells, 3 * chan_in)
            copies[tap].wait()
            part = jnp.dot(window, w_ref[tap * 3 * chan_in : (tap + 1) * 3 * chan_in], preferred_element_type=F32)
            if tap == 0:
                acc_ref[...] = part
            elif tap < 8:
                acc_ref[...] += part
            else:
                o_ref[...] = (acc_ref[...] + part).astype(BF16)


def split_kernel(cut, place, keep_ref, recv_ref, keep1, send1, keep2, send2):
    tm, dp = keep_ref.shape[:2]
    z, x = jnp.bitwise_and(place[0], 1), jnp.bitwise_and(place[2], 1)
    for t in range(tm):
        for j in range(dp // 2):
            mine, other = 2 * j + x, 2 * j + 1 - x
            keep1[t, j] = keep_ref[t, mine, :cut] + recv_ref[t, mine, :cut].astype(F32)
            send1[t, j] = (keep_ref[t, other, :cut] + recv_ref[t, other, :cut].astype(F32)).astype(BF16)
    for j in range(tm // 2):
        for d in range(dp):
            mine, other = 2 * j + z, 2 * j + 1 - z
            keep2[j, d] = keep_ref[mine, d, cut:] + recv_ref[mine, d, cut:].astype(F32)
            send2[j, d] = (keep_ref[other, d, cut:] + recv_ref[other, d, cut:].astype(F32)).astype(BF16)


def bits_of(axis):
    return [1 << k for k in range((lax.axis_size(axis) - 1).bit_length())]


def swap(value, axis, step):
    return lax.ppermute(value, axis, [(i, i ^ step) for i in range(lax.axis_size(axis))])


def after(value, *others):
    return lax.optimization_barrier((value,) + others)[0]


def gather_xor(value, axis):
    value = value[None]
    for step in bits_of(axis):
        value = jnp.concatenate([value, swap(value, axis, step)], axis=0)
    return value


def parts_of(value):
    parts = []
    for _ in range(2):
        part = lax.reduce_precision(value, 8, 7)
        parts.append(part.astype(BF16))
        value = value - part
    return parts + [value.astype(BF16)]


def with_rider(send, rider, axis, step):
    lanes = send.shape[-1]
    load = send.reshape(-1, lanes)
    extra = jnp.concatenate(parts_of(rider), axis=0)
    extra = jnp.pad(extra, ((0, -extra.shape[0] % 16), (0, 0)))
    got = swap(jnp.concatenate([load, extra], axis=0), axis, step)
    n, k = load.shape[0], rider.shape[0]
    parts = [got[n + i * k : n + (i + 1) * k].astype(F32) for i in range(3)]
    return got[:n].reshape(send.shape), rider + ((parts[0] + parts[1]) + parts[2])


def parted(value, axis, step):
    value = value.reshape((value.shape[0] // 2, 2) + value.shape[1:])
    bit = jnp.minimum(jnp.bitwise_and(lax.axis_index(axis), step), 1)
    keep = lax.dynamic_index_in_dim(value, bit, 1, keepdims=False)
    send = lax.dynamic_index_in_dim(value, 1 - bit, 1, keepdims=False)
    return keep, send.astype(BF16)


def body(clips, gain, bias, weight, cotangent):
    x, g = clips[0], cotangent[0]
    frames, rows, cols, chan_in = x.shape
    chan_out = g.shape[-1]
    per_group = chan_in // GROUPS
    tm, dp, width = (lax.axis_size(name) for name in ("tm", "dp", "width"))
    per_frame = float(rows * width * cols * per_group)
    z, core = lax.axis_index("tm"), lax.axis_index("width")
    place = jnp.stack([z, core, lax.axis_index("dp")]).astype(jnp.int32)
    cells = rows * cols
    shape = jax.ShapeDtypeStruct
    flat = x.reshape(frames, cells, chan_in)
    conv_flops = 2 * frames * cells * 27 * chan_in * chan_out

    up = [(i, i + 1) for i in range(tm - 1)]
    down = [(i + 1, i) for i in range(tm - 1)]
    flat_g = g.reshape(frames, cells, chan_out)
    g_next = lax.ppermute(flat_g[:2], "tm", down)
    x_prev = lax.ppermute(flat[frames - 2 :], "tm", up)
    sums = call(functools.partial(sums_kernel, per_group), shape((2 * frames, chan_in), F32), [flat])
    sums = sums + swap(sums, "width", 1)
    stats = gather_xor(sums, "tm")

    def edge_row(value):
        return jnp.where(core == 0, value[:, cells - cols :], value[:, :cols])

    g_edge = swap(jnp.concatenate([edge_row(flat_g), edge_row(g_next)], axis=0), "width", 1)
    x_edge = swap(jnp.concatenate([edge_row(x_prev), edge_row(flat)], axis=0), "width", 1)
    stats, x_prev, x_edge = lax.optimization_barrier((stats, x_prev, x_edge))
    g_next = g_next.reshape(2, rows, cols, chan_out)
    x_prev = x_prev.reshape(2, rows, cols, chan_in)

    norm = [place, stats, gain[None], bias[None]]
    padded = pltpu.VMEM((frames + 2, rows + 2, cols, chan_out), BF16)
    copied = [pltpu.VMEM(weight.shape, BF16), pltpu.SemaphoreType.DMA((9,))]
    half = chan_out // 2
    keep, send = call(
        functools.partial(kernel_grad_kernel, per_frame),
        (shape((27 * chan_in, half), F32), shape((27 * chan_in, half), BF16)),
        norm + [flat, g, g_next, g_edge],
        [padded, pltpu.VMEM((3 * chan_in, frames * cells), BF16)],
        conv_flops,
        1,
    )
    grad_hidden = call(
        grad_hidden_kernel,
        shape((frames * cells, chan_in), F32),
        [place, g, g_next, after(g_edge, send), weight],
        [padded, pltpu.VMEM((frames * cells, 3 * chan_in), F32), *copied],
        conv_flops,
        1,
        1,
    )
    recv = after(swap(send, "width", 1), grad_hidden)
    share = 27 * chan_in // (tm * dp)
    cut = max(share * 11 // 16 // 16 * 16, 1)
    rest = share - cut
    whole = (tm, dp, share, half)
    keep1, send1, keep2, send2 = call(
        functools.partial(split_kernel, cut),
        (
            shape((tm, dp // 2, cut, half), F32),
            shape((tm, dp // 2, cut, half), BF16),
            shape((tm // 2, dp, rest, half), F32),
            shape((tm // 2, dp, rest, half), BF16),
        ),
        [place, keep.reshape(whole), recv.reshape(whole)],
        scalars=1,
    )
    recv2 = swap(send2, "tm", 1)
    recv1 = swap(send1, "dp", 1)
    local = call(
        functools.partial(gain_kernel, per_frame),
        shape((2, chan_in), F32),
        norm + [flat, after(grad_hidden, send1, send2)],
        scalars=1,
    )
    rider = local + swap(local, "width", 1)
    two = keep2 + after(recv2, rider).astype(F32)
    hold = stats
    for step in bits_of("tm")[1:]:
        two, send = parted(two, "tm", step)
        hold = after(hold, send)
        got, rider = with_rider(send, rider, "tm", step)
        two = two + got.astype(F32)
    output = call(
        functools.partial(output_kernel, per_frame),
        shape((frames * cells, chan_out), BF16),
        [place, hold, gain[None], bias[None], x, x_prev, x_edge, weight],
        [
            pltpu.VMEM((frames + 2, rows + 2, cols, 3 * chan_in), BF16),
            pltpu.VMEM((frames * cells, chan_out), F32),
            *copied,
        ],
        conv_flops,
        1,
        1,
    )
    two, rider, recv1, output = lax.optimization_barrier((two, rider, recv1, output))
    one = jnp.moveaxis(keep1 + recv1.astype(F32), 1, 0)
    for step in bits_of("dp")[1:]:
        one, send = parted(one, "dp", step)
        one = one + swap(send, "dp", step).astype(F32)
    one = one[0]
    for step in bits_of("tm"):
        one, send = parted(one, "tm", step)
        if step == 1:
            got, rider = with_rider(send, rider, "tm", step)
        else:
            got = swap(send, "tm", step)
        one = one + got.astype(F32)
    two = two[0]
    for step in bits_of("dp"):
        two, send = parted(two, "dp", step)
        got, rider = with_rider(send, rider, "dp", step)
        two = two + got.astype(F32)
    grad_weight = jnp.concatenate([one[0], two[0]], axis=0)
    return (output.reshape(1, frames, rows, cols, chan_out), grad_weight, rider[0], rider[1])


def solution(mesh):
    return jax.shard_map(
        body,
        mesh=mesh,
        in_specs=(
            P(("groups", "dp"), "tm", "width", None, None),
            P(),
            P(),
            P(),
            P(("groups", "dp"), "tm", "width", None, None),
        ),
        out_specs=(
            P(("groups", "dp"), "tm", "width", None, None),
            P(("groups", "tm", "dp"), "width"),
            P("groups"),
            P("groups"),
        ),
        check_vma=False,
    )
```

```python
import functools

import jax
import jax.numpy as jnp
from jax import lax
from jax.experimental import pallas as pl
from jax.experimental.pallas import tpu as pltpu
from jax.sharding import PartitionSpec as P

GROUPS = 32
OTHERS = (2, 3, 1)
F32, BF16 = jnp.float32, jnp.bfloat16
VMEM = pl.BlockSpec(memory_space=pltpu.VMEM)
SMEM = pl.BlockSpec(memory_space=pltpu.SMEM)
HBM = pl.BlockSpec(memory_space=pltpu.HBM)


def call(kernel, out_shape, inputs, scratch=(), flops=0, scalars=0, far=0):
    outs = jax.tree.leaves(out_shape)
    moved = sum(v.size * v.dtype.itemsize for v in list(inputs) + list(outs))
    return pl.pallas_call(
        kernel,
        out_shape=out_shape,
        in_specs=[SMEM] * scalars + [VMEM] * (len(inputs) - scalars - far) + [HBM] * far,
        out_specs=jax.tree.map(lambda _: VMEM, out_shape),
        scratch_shapes=list(scratch),
        cost_estimate=pl.CostEstimate(flops=0, bytes_accessed=moved, transcendentals=0),
        compiler_params=pltpu.CompilerParams(vmem_limit_bytes=16 << 20),
    )(*inputs)


def far(value):
    return pltpu.with_memory_space_constraint(value, pltpu.HBM)


def group_sum(rows, per_group):
    lane = lax.broadcasted_iota(jnp.int32, rows.shape, 1)
    lanes = rows.shape[1]
    step = 1
    while step < per_group:
        up = pltpu.roll(rows, lanes - step, 1)
        down = pltpu.roll(rows, step, 1)
        rows = rows + jnp.where((lane // step) % 2 == 0, up, down)
        step *= 2
    return rows


def prepare_kernel(per_group, place, x_hbm, g_hbm, sums_ref, last_ref, row_ref, x_row_ref, x_ref, sems):
    frames, rows, cols, chan_in = x_ref.shape
    row = jnp.where(place[1] == 0, rows - 1, 0)
    copies = [pltpu.make_async_copy(x_hbm.at[t], x_ref.at[t], sems.at[t]) for t in range(frames)]
    copies += [pltpu.make_async_copy(g_hbm.at[t, row], row_ref.at[t], sems.at[frames + t]) for t in range(frames)]
    for copy in copies:
        copy.start()
    firsts, squares = [], []
    for t in range(frames):
        copies[t].wait()
        v = x_ref[t].reshape(rows * cols, chan_in).astype(F32)
        firsts.append(jnp.sum(v, axis=0, keepdims=True))
        squares.append(jnp.sum(v * v, axis=0, keepdims=True))
        x_row_ref[t] = x_ref[t, row]
    last_ref[...] = x_ref[frames - 2 :]
    sums_ref[...] = group_sum(jnp.concatenate(firsts + squares, axis=0), per_group)
    for copy in copies[frames:]:
        copy.wait()


def edge_kernel(place, first_ref, *rest):
    o_ref = rest[-1]
    row = jnp.where(place[1] == 0, first_ref.shape[1] - 1, 0)
    at = 0
    for ref in (first_ref,) + rest[:-1]:
        for t in range(ref.shape[0]):
            o_ref[at + t] = ref[t, row]
        at += ref.shape[0]


def frame_stats(place, stats_ref, frames, per_frame):
    devices = stats_ref.shape[0] - 1
    mine = place[0]
    own = stats_ref[0]
    before = jnp.zeros_like(own)
    behind = jnp.zeros_like(own)
    for x in range(1, devices):
        other = jnp.bitwise_xor(mine, x)
        rows = stats_ref[x]
        before = before + jnp.where(other < mine - 1, rows, 0.0)
        behind = behind + jnp.where(other == mine - 1, rows, 0.0)

    def total(rows, at):
        return jnp.sum(rows[at : at + frames], axis=0, keepdims=True)

    first, square = total(before, 0), total(before, frames)
    means, inverses = [], []
    for k in range(2 * frames):
        rows, t = (behind, k) if k < frames else (own, k - frames)
        first = first + rows[t : t + 1]
        square = square + rows[frames + t : frames + t + 1]
        if k < frames - 2:
            continue
        shown = jnp.maximum(mine * frames + k - frames + 1, 1).astype(F32) * per_frame
        mean = first / shown
        variance = square / shown - mean * mean
        means.append(mean)
        inverses.append(lax.rsqrt(variance + 1e-05))
    return means, inverses


def pad_rows(core, own, edge, dst):
    rows = own.shape[1]
    zero = jnp.zeros_like(edge)
    dst[:, 0] = jnp.where(core == 0, zero, edge)
    dst[:, rows + 1] = jnp.where(core == 0, edge, zero)
    dst[:, 1 : rows + 1] = own


def by_taps(window, w_ref, tap, chan_in):
    size = 3 * chan_in
    start = tap * size if isinstance(tap, int) else pl.multiple_of(tap * size, size)
    return lax.dot_general(
        window, w_ref[pl.ds(start, size)], (((1,), (1,)), ((), ())), preferred_element_type=F32
    )


def own_grad_kernel(g_ref, w_ref, z_ref, gp_ref):
    frames, rows, cols, chan_out = g_ref.shape
    chan_in = z_ref.shape[3] // 3
    zero = jnp.zeros((frames, cols, chan_out), BF16)
    gp_ref[:, 0] = zero
    gp_ref[:, rows + 1] = zero
    gp_ref[:, 1 : rows + 1] = g_ref[...]
    for a in (2, 1, 0):
        n = frames - 2 + a
        for b in range(3):
            window = gp_ref[2 - a :, 2 - b : 2 - b + rows].reshape(n * rows * cols, chan_out)
            part = by_taps(window, w_ref, a * 3 + b, chan_in).reshape(n, rows, cols, 3 * chan_in)
            if a == 2 and b == 0:
                z_ref[...] = part
            else:
                z_ref[:n] += part


def gain_kernel(
    per_frame, place, stats_ref, x_ref, own_ref, next_ref, edge_ref, edge_next, w_ref, o_ref, gp_ref, z_ref
):
    frames, rows, cols, chan_out = own_ref.shape[:3] + (next_ref.shape[3],)
    chan_in = x_ref.shape[2]
    cells = rows * cols
    core = place[1]
    pad_rows(core, next_ref[...], edge_next[...], gp_ref)
    z_ref[...] = own_ref[...]
    for a in range(2):
        n = 2 - a
        for b in range(3):
            window = gp_ref[:n, 2 - b : 2 - b + rows].reshape(n * cells, chan_out)
            part = by_taps(window, w_ref, a * 3 + b, chan_in).reshape(n, rows, cols, 3 * chan_in)
            z_ref[frames - n :] += part
    row = jnp.where(core == 0, rows - 1, 0)
    tap_row = jnp.where(core == 0, 0, 2)
    for a in range(3):
        n = frames - 2 + a
        window = edge_ref[2 - a : frames].reshape(n * cols, chan_out)
        part = by_taps(window, w_ref, a * 3 + tap_row, chan_in)
        for t in range(n):
            z_ref[t, row] += part[t * cols : (t + 1) * cols]
    means, inverses = frame_stats(place, stats_ref, frames, per_frame)
    affine = stats_ref[stats_ref.shape[0] - 1]
    gain, bias = affine[:1], affine[1:2]
    col = lax.broadcasted_iota(jnp.int32, (cells, chan_in), 0) % cols
    by_gain = jnp.zeros((1, chan_in), F32)
    by_bias = jnp.zeros((1, chan_in), F32)
    for t in range(frames):
        z = z_ref[t].reshape(cells, 3 * chan_in)
        left = jnp.where(col == cols - 1, 0.0, pltpu.roll(z[:, :chan_in], cells - 1, 0))
        right = jnp.where(col == 0, 0.0, pltpu.roll(z[:, 2 * chan_in :], 1, 0))
        grad_hidden = left + z[:, chan_in : 2 * chan_in] + right
        normed = (x_ref[t].astype(F32) - means[2 + t]) * inverses[2 + t]
        act = normed * gain + bias
        sigma = lax.logistic(act)
        grad_act = grad_hidden * sigma * (1.0 + act * (1.0 - sigma))
        by_gain = by_gain + jnp.sum(grad_act * normed, axis=0, keepdims=True)
        by_bias = by_bias + jnp.sum(grad_act, axis=0, keepdims=True)
    o_ref[...] = jnp.concatenate([by_gain, by_bias], axis=0)


def kernel_grad_kernel(
    per_frame, late, skip, place, stats_ref, next_ref, edge_ref, edge_next, x_hbm, g_hbm, *rest
):
    keep_ref, send_ref, ht_ref, gp_ref, x_ref, g_ref, sems = rest
    frames, cells, chan_in = x_ref.shape
    rows, cols, chan_out = g_ref.shape[1:]
    core = place[1]
    copies = [pltpu.make_async_copy(x_hbm.at[t], x_ref.at[t], sems.at[t]) for t in range(frames)]
    copies.append(pltpu.make_async_copy(g_hbm, g_ref, sems.at[frames]))
    for copy in copies:
        copy.start()
    pad_rows(core, next_ref[...], edge_next[...], gp_ref.at[frames:])
    means, inverses = frame_stats(place, stats_ref, frames, per_frame)
    affine = stats_ref[stats_ref.shape[0] - 1]
    gain, bias = affine[:1], affine[1:2]
    block = 2 * cols
    lane = lax.broadcasted_iota(jnp.int32, (chan_in, block), 1) % cols
    for t in range(frames):
        copies[t].wait()
        for half in range(cells // block):
            v = x_ref[t, half * block : (half + 1) * block].astype(F32)
            act = (v - means[2 + t]) * inverses[2 + t] * gain + bias
            hidden = (act * lax.logistic(act)).astype(BF16).astype(F32)
            turned = hidden.T
            at = t * cells + half * block
            earlier = jnp.where(lane == 0, 0.0, pltpu.roll(turned, 1, 1))
            later = jnp.where(lane == cols - 1, 0.0, pltpu.roll(turned, block - 1, 1))
            for d, piece in enumerate((earlier, turned, later)):
                piece = piece.astype(BF16)
                for k in range(chan_in // 16):
                    to = late(d * (chan_in // 16) + k) * 16
                    ht_ref[to : to + 16, at : at + block] = piece[k * 16 : (k + 1) * 16]
    copies[frames].wait()
    pad_rows(core, g_ref[...], edge_ref[...], gp_ref.at[:frames])
    mine = chan_out // 2
    n = 3 * chan_in
    for a in range(3):
        for b in range(3):
            tap = a * 3 + b
            window = gp_ref[2 - a : 2 - a + frames, 2 - b : 2 - b + rows].reshape(frames * cells, chan_out)
            part = jnp.dot(ht_ref[...], window, preferred_element_type=F32)
            low, high = part[:, :mine], part[:, mine:]
            keep = jnp.where(core == 0, low, high)
            send = jnp.where(core == 0, high, low).astype(BF16)
            for begin, end, at in ((0, skip, tap * skip), (skip, n, 9 * skip + tap * (n - skip))):
                if end > begin:
                    keep_ref[at : at + end - begin] = keep[begin:end]
                    send_ref[at : at + end - begin] = send[begin:end]


def output_kernel(
    per_frame, place, stats_ref, x_ref, prev_ref, edge_ref, prev_edge, w_ref, o_ref, h_ref, acc_ref
):
    frames, rows, cols, chan_in = x_ref.shape
    begin, count = 0, frames
    mine, core = place[0], place[1]
    means, inverses = frame_stats(place, stats_ref, frames, per_frame)
    affine = stats_ref[stats_ref.shape[0] - 1]
    gain, bias = affine[:1], affine[1:2]

    def put(f, r0, rows_now, value, keep):
        act = (value.astype(F32) - means[f]) * inverses[f] * gain + bias
        hidden = act * lax.logistic(act)
        if keep is not None:
            hidden = jnp.where(keep, hidden, 0.0)
        n = rows_now * cols
        col = lax.broadcasted_iota(jnp.int32, (n, chan_in), 0) % cols
        earlier = jnp.where(col == 0, 0.0, pltpu.roll(hidden, 1, 0))
        later = jnp.where(col == cols - 1, 0.0, pltpu.roll(hidden, n - 1, 0))
        for d, piece in enumerate((earlier, hidden, later)):
            h_ref[f - begin, r0 : r0 + rows_now, :, d * chan_in : (d + 1) * chan_in] = piece.astype(BF16).reshape(
                rows_now, cols, chan_in
            )

    for f in range(begin, begin + count + 2):
        inside = (mine > 0) if f < 2 else None
        value = prev_ref[f] if f < 2 else x_ref[f - 2]
        put(f, 1, rows, value.reshape(rows * cols, chan_in), inside)
        for r0, here in ((0, core == 1), (rows + 1, core == 0)):
            put(f, r0, 1, prev_edge[f] if f < 2 else edge_ref[f - 2], here if inside is None else jnp.logical_and(here, inside))
    cells = count * rows * cols
    for a in range(3):
        for b in range(3):
            tap = a * 3 + b
            window = h_ref[a : a + count, b : b + rows].reshape(cells, 3 * chan_in)
            part = jnp.dot(window, w_ref[tap * 3 * chan_in : (tap + 1) * 3 * chan_in], preferred_element_type=F32)
            if tap == 0:
                acc_ref[...] = part
            elif tap < 8:
                acc_ref[...] += part
            else:
                o_ref[...] = (acc_ref[...] + part).astype(BF16)


def split_kernel(cut, rest, place, keep_ref, recv_ref, stay1, send1, stay2, *send2):
    tm = len(send2) + 1

    def total(at):
        rows = pl.ds(pl.multiple_of(at, 16), size)
        return keep_ref[rows] + recv_ref[rows].astype(F32)

    size = rest
    stay2[...] = total(place[0] * rest)
    for k, send in zip(OTHERS, send2):
        send[...] = total(jnp.bitwise_xor(place[0], k) * rest).astype(BF16)
    size = cut
    for t in range(tm):
        at = tm * rest + 2 * t * cut
        stay1[t * cut : (t + 1) * cut] = total(at + place[2] * cut)
        send1[t * cut : (t + 1) * cut] = total(at + (1 - place[2]) * cut).astype(BF16)


def put_rider(rider, dst, at):
    parts = []
    for _ in range(3):
        part = rider.astype(BF16)
        rider = rider - part.astype(F32)
        parts.append(part.astype(F32))
    parts.append(jnp.zeros((16 - 3 * rider.shape[0], rider.shape[1]), F32))
    dst[at : at + 16] = jnp.concatenate(parts, axis=0).astype(BF16)


def get_rider(src, at, n):
    rows = src[at : at + 16].astype(F32)
    return (rows[:n] + rows[n : 2 * n]) + rows[2 * n : 3 * n]


def middle_kernel(place, stay1_ref, recv1_ref, stay2_ref, b_ref, c_ref, a_ref, rider_ref, got_ref, *outs):
    stay1, sends, stay2, send2, rider_out = outs[0], outs[1:4], outs[4], outs[5], outs[6]
    rider = rider_ref[...] + got_ref[...]
    rider_out[...] = rider
    n = stay1.shape[0]

    def total(other):
        rows = pl.ds(pl.multiple_of(jnp.bitwise_xor(place[0], other) * n, 16), n)
        return stay1_ref[rows] + recv1_ref[rows].astype(F32)

    stay1[...] = total(0)
    for k, send in zip(OTHERS, sends):
        send[:n] = total(k).astype(BF16)
        put_rider(rider, send, n)
    m = stay2.shape[0]

    def summed(bit):
        rows = pl.ds(pl.multiple_of(bit * m, 16), m)
        first = stay2_ref[rows] + a_ref[rows].astype(F32)
        return first + (b_ref[rows].astype(F32) + c_ref[rows].astype(F32))

    stay2[...] = summed(place[2])
    send2[...] = summed(1 - place[2]).astype(BF16)


def last_kernel(stay1_ref, b_ref, c_ref, a_ref, stay2_ref, recv2_ref, rider_ref, o_ref, gain_ref, bias_ref):
    for k in range(stay2_ref.shape[0] // 16):
        two, one = slice(16 * k, 16 * k + 16), slice(32 * k, 32 * k + 32)
        near = stay1_ref[one] + a_ref[one].astype(F32)
        o_ref[48 * k : 48 * k + 32] = near + (b_ref[one].astype(F32) + c_ref[one].astype(F32))
        o_ref[48 * k + 32 : 48 * k + 48] = stay2_ref[two] + recv2_ref[two].astype(F32)
    n = stay1_ref.shape[0]
    near, b, c = (get_rider(ref, n, 2) for ref in (a_ref, b_ref, c_ref))
    rider = (rider_ref[...] + near) + (b + c)
    gain_ref[...] = rider[:1]
    bias_ref[...] = rider[1:]


def bits_of(axis):
    return [1 << k for k in range((lax.axis_size(axis) - 1).bit_length())]


def swap(value, axis, step):
    return lax.ppermute(value, axis, [(i, i ^ step) for i in range(lax.axis_size(axis))])


def together(*values):
    return lax.optimization_barrier(values)


def all_sum(value, axes):
    for axis in axes:
        for step in bits_of(axis):
            value = value + swap(value, axis, step)
    return value


def parted(value, axis, step):
    value = value.reshape((value.shape[0] // 2, 2) + value.shape[1:])
    bit = jnp.minimum(jnp.bitwise_and(lax.axis_index(axis), step), 1)
    keep = lax.dynamic_index_in_dim(value, bit, 1, keepdims=False)
    send = lax.dynamic_index_in_dim(value, 1 - bit, 1, keepdims=False)
    return keep, send.astype(BF16)


def body(clips, gain, bias, weight, cotangent):
    x, g = clips[0], cotangent[0]
    frames, rows, cols, chan_in = x.shape
    chan_out = g.shape[-1]
    per_group = chan_in // GROUPS
    tm, dp, width = (lax.axis_size(name) for name in ("tm", "dp", "width"))
    per_frame = float(rows * width * cols * per_group)
    z, core = lax.axis_index("tm"), lax.axis_index("width")
    place = jnp.stack([z, core, lax.axis_index("dp")]).astype(jnp.int32)
    cells = rows * cols
    shape = jax.ShapeDtypeStruct
    half = chan_out // 2

    up = [(i, i + 1) for i in range(tm - 1)]
    down = [(i + 1, i) for i in range(tm - 1)]
    affine = jnp.pad(jnp.stack([gain, bias]), ((0, 2 * frames - 2), (0, 0)))[None]
    x, g, place = together(x, g, place)
    g_first = g.reshape(frames, cells, chan_out)[:2]
    flat = x.reshape(frames, cells, chan_in)
    g_next = lax.ppermute(g_first, "tm", down).reshape(2, rows, cols, chan_out)
    sums, x_last, g_rows, x_rows = call(
        functools.partial(prepare_kernel, per_group),
        (
            shape((2 * frames, chan_in), F32),
            shape((2, rows, cols, chan_in), BF16),
            shape((frames, cols, chan_out), BF16),
            shape((frames, cols, chan_in), BF16),
        ),
        [place, far(x), far(g)],
        [pltpu.VMEM(x.shape, BF16), pltpu.SemaphoreType.DMA((2 * frames,))],
        scalars=1,
        far=2,
    )
    sums = sums + swap(sums, "width", 1)
    g_edge = swap(g_rows, "width", 1)
    x_edge = swap(x_rows, "width", 1)
    sums, g_next, g_edge, x_edge = together(sums, g_next, g_edge, x_edge)

    def edges(*values):
        rows_out = (sum(v.shape[0] for v in values), cols, values[0].shape[3])
        return call(edge_kernel, shape(rows_out, BF16), [place, *values], scalars=1)

    next_edge = swap(edges(g_next), "width", 1)
    stats = sums[None]
    for step in bits_of("tm"):
        stats = jnp.concatenate([stats, swap(stats, "tm", step)], axis=0)
    stats = jnp.concatenate([stats, affine], axis=0)
    stats, next_edge = together(stats, next_edge)

    share = 27 * chan_in // (tm * dp)
    pieces = share % 48 == 0 and tm == 4 and dp == 2
    count = 3 * chan_in // 48
    if pieces:
        skip = chan_in
        late = lambda k: k // 3 if k % 3 == 2 else count + k // 3 * 2 + k % 3
    else:
        skip = 0
        late = lambda k: k
    keep, send = call(
        functools.partial(kernel_grad_kernel, per_frame, late, skip),
        (shape((27 * chan_in, half), F32), shape((27 * chan_in, half), BF16)),
        [place, stats, g_next, g_edge, next_edge, far(flat), far(g)],
        [
            pltpu.VMEM((3 * chan_in, frames * cells), BF16),
            pltpu.VMEM((frames + 2, rows + 2, cols, chan_out), BF16),
            pltpu.VMEM(flat.shape, BF16),
            pltpu.VMEM(g.shape, BF16),
            pltpu.SemaphoreType.DMA((frames + 1,)),
        ],
        scalars=1,
        far=2,
    )
    recv = swap(send, "width", 1)
    send, x_last, x_rows = together(send, x_last, x_rows)
    x_prev = lax.ppermute(x_last, "tm", [(i, (i + 1) % tm) for i in range(tm)])
    turn = [(i * width + c, (i + 1) % tm * width + (c ^ 1)) for i in range(tm) for c in range(width)]
    prev_edge = lax.ppermute(x_rows[frames - 2 :], ("tm", "width"), turn)

    def own(g):
        return call(
            own_grad_kernel,
            shape((frames, rows, cols, 3 * chan_in), F32),
            [g, weight],
            [pltpu.VMEM((frames, rows + 2, cols, chan_out), BF16)],
        )

    def gains(stats, own_grad):
        return call(
            functools.partial(gain_kernel, per_frame),
            shape((2, chan_in), F32),
            [place, stats, flat, own_grad, g_next, g_edge, next_edge, weight],
            [
                pltpu.VMEM((2, rows + 2, cols, chan_out), BF16),
                pltpu.VMEM((frames, rows, cols, 3 * chan_in), F32),
            ],
            scalars=1,
        )

    def outputs(hold):
        return call(
            functools.partial(output_kernel, per_frame),
            shape((frames * cells, chan_out), BF16),
            [place, hold, x, x_prev, x_edge, prev_edge, weight],
            [
                pltpu.VMEM((frames + 2, rows + 2, cols, 3 * chan_in), BF16),
                pltpu.VMEM((frames * cells, chan_out), F32),
            ],
            scalars=1,
        )

    if not pieces:
        output = outputs(stats)
        one = keep + recv.astype(F32)
        one = jnp.moveaxis(one.reshape(tm, dp, share, half), 1, 0)
        for step in bits_of("dp"):
            one, send = parted(one, "dp", step)
            one = one + swap(send, "dp", step).astype(F32)
        one = one[0]
        for step in bits_of("tm"):
            one, send = parted(one, "tm", step)
            one = one + swap(send, "tm", step).astype(F32)
        rider = all_sum(gains(stats, own(g)), ("width", "dp", "tm"))
        grad_weight = one[0]
    else:
        rest = share // 3
        cut = share - rest

        def piece(n, kind):
            return shape((n, half), kind)

        both = dp * rest
        stay1, send1, stay2, *send2 = call(
            functools.partial(split_kernel, cut, both),
            [piece(tm * cut, F32), piece(tm * cut, BF16), piece(both, F32)] + [piece(both, BF16)] * (tm - 1),
            [place, keep, recv],
            scalars=1,
        )
        send1, hold, x_prev, prev_edge, g, *send2 = together(send1, stats, x_prev, prev_edge, g, *send2)
        recv1 = swap(send1, "dp", 1)
        recv2 = [swap(v, "tm", k) for k, v in zip(OTHERS, send2)]
        rider = gains(hold, own(g))
        rider = rider + swap(rider, "width", 1)
        rider, hold = together(rider, hold)
        got = swap(rider, "dp", 1)
        recv1, got, *recv2 = together(recv1, got, *recv2)
        stay1, *send1, stay2, send2, rider = call(
            middle_kernel,
            [piece(cut, F32)]
            + [piece(cut + 16, BF16)] * (tm - 1)
            + [piece(rest, F32), piece(rest, BF16), shape(rider.shape, F32)],
            [place, stay1, recv1, stay2, *recv2, rider, got],
            scalars=1,
        )
        send2, hold, *send1 = together(send2, hold, *send1)
        recv1 = [swap(v, "tm", k) for k, v in zip(OTHERS, send1)]
        recv2 = swap(send2, "dp", 1)
        output = outputs(hold)
        recv2, output, *recv1 = together(recv2, output, *recv1)
        row = shape((1, chan_in), F32)
        grad_weight, *rider = call(
            last_kernel, [piece(share, F32), row, row], [stay1, *recv1, stay2, recv2, rider]
        )
        rider = [v.reshape(chan_in) for v in rider]
    return (output.reshape(1, frames, rows, cols, chan_out), grad_weight, rider[0], rider[1])


def solution(mesh):
    return jax.shard_map(
        body,
        mesh=mesh,
        in_specs=(
            P(("groups", "dp"), "tm", "width", None, None),
            P(),
            P(),
            P(),
            P(("groups", "dp"), "tm", "width", None, None),
        ),
        out_specs=(
            P(("groups", "dp"), "tm", "width", None, None),
            P(("groups", "tm", "dp"), "width"),
            P("groups"),
            P("groups"),
        ),
        check_vma=False,
    )
```

```python
import functools

import jax
import jax.numpy as jnp
from jax import lax
from jax.experimental import pallas as pl
from jax.experimental.pallas import tpu as pltpu
from jax.sharding import PartitionSpec as P

GROUPS = 32
OTHERS = (2, 3, 1)
F32, BF16 = jnp.float32, jnp.bfloat16
VMEM = pl.BlockSpec(memory_space=pltpu.VMEM)
SMEM = pl.BlockSpec(memory_space=pltpu.SMEM)
HBM = pl.BlockSpec(memory_space=pltpu.HBM)


def call(kernel, out_shape, inputs, scratch=(), flops=0, scalars=0, far=0):
    outs = jax.tree.leaves(out_shape)
    moved = sum(v.size * v.dtype.itemsize for v in list(inputs) + list(outs))
    return pl.pallas_call(
        kernel,
        out_shape=out_shape,
        in_specs=[SMEM] * scalars + [VMEM] * (len(inputs) - scalars - far) + [HBM] * far,
        out_specs=jax.tree.map(lambda _: VMEM, out_shape),
        scratch_shapes=list(scratch),
        cost_estimate=pl.CostEstimate(flops=0, bytes_accessed=moved, transcendentals=0),
        compiler_params=pltpu.CompilerParams(vmem_limit_bytes=16 << 20),
    )(*inputs)


def far(value):
    return pltpu.with_memory_space_constraint(value, pltpu.HBM)


def group_sum(rows, per_group):
    lane = lax.broadcasted_iota(jnp.int32, rows.shape, 1)
    lanes = rows.shape[1]
    step = 1
    while step < per_group:
        up = pltpu.roll(rows, lanes - step, 1)
        down = pltpu.roll(rows, step, 1)
        rows = rows + jnp.where((lane // step) % 2 == 0, up, down)
        step *= 2
    return rows


def prepare_kernel(per_group, place, x_hbm, g_hbm, sums_ref, last_ref, row_ref, x_row_ref, x_ref, g_ref, sems):
    frames, rows, cols, chan_in = x_ref.shape
    row = jnp.where(place[1] == 0, rows - 1, 0)
    copies = [pltpu.make_async_copy(x_hbm.at[t], x_ref.at[t], sems.at[t]) for t in range(frames)]
    copies += [pltpu.make_async_copy(g_hbm.at[t], g_ref.at[t], sems.at[frames + t]) for t in range(frames)]
    for copy in copies:
        copy.start()
    firsts, squares = [], []
    for t in range(frames):
        copies[t].wait()
        v = x_ref[t].reshape(rows * cols, chan_in).astype(F32)
        firsts.append(jnp.sum(v, axis=0, keepdims=True))
        squares.append(jnp.sum(v * v, axis=0, keepdims=True))
        x_row_ref[t] = x_ref[t, row]
    last_ref[...] = x_ref[frames - 2 :]
    sums_ref[...] = group_sum(jnp.concatenate(firsts + squares, axis=0), per_group)
    for t in range(frames):
        copies[frames + t].wait()
        row_ref[t] = g_ref[t, row]


def edge_kernel(place, first_ref, *rest):
    o_ref = rest[-1]
    row = jnp.where(place[1] == 0, first_ref.shape[1] - 1, 0)
    at = 0
    for ref in (first_ref,) + rest[:-1]:
        for t in range(ref.shape[0]):
            o_ref[at + t] = ref[t, row]
        at += ref.shape[0]


def frame_stats(place, stats_ref, frames, per_frame):
    devices = stats_ref.shape[0] - 1
    mine = place[0]
    own = stats_ref[0]
    before = jnp.zeros_like(own)
    behind = jnp.zeros_like(own)
    for x in range(1, devices):
        other = jnp.bitwise_xor(mine, x)
        rows = stats_ref[x]
        before = before + jnp.where(other < mine - 1, rows, 0.0)
        behind = behind + jnp.where(other == mine - 1, rows, 0.0)

    def total(rows, at):
        return jnp.sum(rows[at : at + frames], axis=0, keepdims=True)

    first, square = total(before, 0), total(before, frames)
    means, inverses = [], []
    for k in range(2 * frames):
        rows, t = (behind, k) if k < frames else (own, k - frames)
        first = first + rows[t : t + 1]
        square = square + rows[frames + t : frames + t + 1]
        if k < frames - 2:
            continue
        shown = jnp.maximum(mine * frames + k - frames + 1, 1).astype(F32) * per_frame
        mean = first / shown
        variance = square / shown - mean * mean
        means.append(mean)
        inverses.append(lax.rsqrt(variance + 1e-05))
    return means, inverses


def pad_rows(core, own, edge, dst):
    rows = own.shape[1]
    zero = jnp.zeros_like(edge)
    dst[:, 0] = jnp.where(core == 0, zero, edge)
    dst[:, rows + 1] = jnp.where(core == 0, edge, zero)
    dst[:, 1 : rows + 1] = own


def by_taps(window, w_ref, tap, chan_in):
    size = 3 * chan_in
    start = tap * size if isinstance(tap, int) else pl.multiple_of(tap * size, size)
    return lax.dot_general(
        window, w_ref[pl.ds(start, size)], (((1,), (1,)), ((), ())), preferred_element_type=F32
    )


def own_grad_kernel(g_ref, w_ref, z_ref, gp_ref):
    frames, rows, cols, chan_out = g_ref.shape
    chan_in = z_ref.shape[3] // 3
    zero = jnp.zeros((frames, cols, chan_out), BF16)
    gp_ref[:, 0] = zero
    gp_ref[:, rows + 1] = zero
    gp_ref[:, 1 : rows + 1] = g_ref[...]
    for a in (2, 1, 0):
        n = frames - 2 + a
        for b in range(3):
            window = gp_ref[2 - a :, 2 - b : 2 - b + rows].reshape(n * rows * cols, chan_out)
            part = by_taps(window, w_ref, a * 3 + b, chan_in).reshape(n, rows, cols, 3 * chan_in)
            if a == 2 and b == 0:
                z_ref[...] = part
            else:
                z_ref[:n] += part


def gain_kernel(
    per_frame, place, stats_ref, x_ref, own_ref, next_ref, edge_ref, edge_next, w_ref, o_ref, gp_ref, z_ref
):
    frames, rows, cols, chan_out = own_ref.shape[:3] + (next_ref.shape[3],)
    chan_in = x_ref.shape[2]
    cells = rows * cols
    core = place[1]
    pad_rows(core, next_ref[...], edge_next[...], gp_ref)
    z_ref[...] = own_ref[...]
    for a in range(2):
        n = 2 - a
        for b in range(3):
            window = gp_ref[:n, 2 - b : 2 - b + rows].reshape(n * cells, chan_out)
            part = by_taps(window, w_ref, a * 3 + b, chan_in).reshape(n, rows, cols, 3 * chan_in)
            z_ref[frames - n :] += part
    row = jnp.where(core == 0, rows - 1, 0)
    tap_row = jnp.where(core == 0, 0, 2)
    for a in range(3):
        n = frames - 2 + a
        window = edge_ref[2 - a : frames].reshape(n * cols, chan_out)
        part = by_taps(window, w_ref, a * 3 + tap_row, chan_in)
        for t in range(n):
            z_ref[t, row] += part[t * cols : (t + 1) * cols]
    means, inverses = frame_stats(place, stats_ref, frames, per_frame)
    affine = stats_ref[stats_ref.shape[0] - 1]
    gain, bias = affine[:1], affine[1:2]
    col = lax.broadcasted_iota(jnp.int32, (cells, chan_in), 0) % cols
    by_gain = jnp.zeros((1, chan_in), F32)
    by_bias = jnp.zeros((1, chan_in), F32)
    for t in range(frames):
        z = z_ref[t].reshape(cells, 3 * chan_in)
        left = jnp.where(col == cols - 1, 0.0, pltpu.roll(z[:, :chan_in], cells - 1, 0))
        right = jnp.where(col == 0, 0.0, pltpu.roll(z[:, 2 * chan_in :], 1, 0))
        grad_hidden = left + z[:, chan_in : 2 * chan_in] + right
        normed = (x_ref[t].astype(F32) - means[2 + t]) * inverses[2 + t]
        act = normed * gain + bias
        sigma = lax.logistic(act)
        grad_act = grad_hidden * sigma * (1.0 + act * (1.0 - sigma))
        by_gain = by_gain + jnp.sum(grad_act * normed, axis=0, keepdims=True)
        by_bias = by_bias + jnp.sum(grad_act, axis=0, keepdims=True)
    o_ref[...] = jnp.concatenate([by_gain, by_bias], axis=0)


def kernel_grad_kernel(
    per_frame, late, skip, place, stats_ref, next_ref, edge_ref, edge_next, x_ref, g_ref, *rest
):
    keep_ref, send_ref, ht_ref, gp_ref = rest
    frames, cells, chan_in = x_ref.shape
    rows, cols, chan_out = g_ref.shape[1:]
    core = place[1]
    pad_rows(core, g_ref[...], edge_ref[...], gp_ref.at[:frames])
    pad_rows(core, next_ref[...], edge_next[...], gp_ref.at[frames:])
    means, inverses = frame_stats(place, stats_ref, frames, per_frame)
    affine = stats_ref[stats_ref.shape[0] - 1]
    gain, bias = affine[:1], affine[1:2]
    block = 2 * cols
    lane = lax.broadcasted_iota(jnp.int32, (chan_in, block), 1) % cols
    for t in range(frames):
        for half in range(cells // block):
            v = x_ref[t, half * block : (half + 1) * block].astype(F32)
            act = (v - means[2 + t]) * inverses[2 + t] * gain + bias
            hidden = (act * lax.logistic(act)).astype(BF16).astype(F32)
            turned = hidden.T
            at = t * cells + half * block
            earlier = jnp.where(lane == 0, 0.0, pltpu.roll(turned, 1, 1))
            later = jnp.where(lane == cols - 1, 0.0, pltpu.roll(turned, block - 1, 1))
            for d, piece in enumerate((earlier, turned, later)):
                piece = piece.astype(BF16)
                for k in range(chan_in // 16):
                    to = late(d * (chan_in // 16) + k) * 16
                    ht_ref[to : to + 16, at : at + block] = piece[k * 16 : (k + 1) * 16]
    mine = chan_out // 2
    n = 3 * chan_in
    for a in range(3):
        for b in range(3):
            tap = a * 3 + b
            window = gp_ref[2 - a : 2 - a + frames, 2 - b : 2 - b + rows].reshape(frames * cells, chan_out)
            part = jnp.dot(ht_ref[...], window, preferred_element_type=F32)
            low, high = part[:, :mine], part[:, mine:]
            keep = jnp.where(core == 0, low, high)
            send = jnp.where(core == 0, high, low).astype(BF16)
            for begin, end, at in ((0, skip, tap * skip), (skip, n, 9 * skip + tap * (n - skip))):
                if end > begin:
                    keep_ref[at : at + end - begin] = keep[begin:end]
                    send_ref[at : at + end - begin] = send[begin:end]


def output_kernel(
    per_frame, place, stats_ref, x_ref, prev_ref, edge_ref, prev_edge, w_ref, o_ref, h_ref, acc_ref
):
    frames, rows, cols, chan_in = x_ref.shape
    begin, count = 0, frames
    mine, core = place[0], place[1]
    means, inverses = frame_stats(place, stats_ref, frames, per_frame)
    affine = stats_ref[stats_ref.shape[0] - 1]
    gain, bias = affine[:1], affine[1:2]

    def put(f, r0, rows_now, value, keep):
        act = (value.astype(F32) - means[f]) * inverses[f] * gain + bias
        hidden = act * lax.logistic(act)
        if keep is not None:
            hidden = jnp.where(keep, hidden, 0.0)
        n = rows_now * cols
        col = lax.broadcasted_iota(jnp.int32, (n, chan_in), 0) % cols
        earlier = jnp.where(col == 0, 0.0, pltpu.roll(hidden, 1, 0))
        later = jnp.where(col == cols - 1, 0.0, pltpu.roll(hidden, n - 1, 0))
        for d, piece in enumerate((earlier, hidden, later)):
            h_ref[f - begin, r0 : r0 + rows_now, :, d * chan_in : (d + 1) * chan_in] = piece.astype(BF16).reshape(
                rows_now, cols, chan_in
            )

    for f in range(begin, begin + count + 2):
        inside = (mine > 0) if f < 2 else None
        value = prev_ref[f] if f < 2 else x_ref[f - 2]
        put(f, 1, rows, value.reshape(rows * cols, chan_in), inside)
        for r0, here in ((0, core == 1), (rows + 1, core == 0)):
            put(f, r0, 1, prev_edge[f] if f < 2 else edge_ref[f - 2], here if inside is None else jnp.logical_and(here, inside))
    cells = count * rows * cols
    for a in range(3):
        for b in range(3):
            tap = a * 3 + b
            window = h_ref[a : a + count, b : b + rows].reshape(cells, 3 * chan_in)
            part = jnp.dot(window, w_ref[tap * 3 * chan_in : (tap + 1) * 3 * chan_in], preferred_element_type=F32)
            if tap == 0:
                acc_ref[...] = part
            elif tap < 8:
                acc_ref[...] += part
            else:
                o_ref[...] = (acc_ref[...] + part).astype(BF16)


def split_kernel(cut, rest, place, keep_ref, recv_ref, stay1, send1, stay2, *send2):
    tm = len(send2) + 1

    def total(at):
        rows = pl.ds(pl.multiple_of(at, 16), size)
        return keep_ref[rows] + recv_ref[rows].astype(F32)

    size = rest
    stay2[...] = total(place[0] * rest)
    for k, send in zip(OTHERS, send2):
        send[...] = total(jnp.bitwise_xor(place[0], k) * rest).astype(BF16)
    size = cut
    for t in range(tm):
        at = tm * rest + 2 * t * cut
        stay1[t * cut : (t + 1) * cut] = total(at + place[2] * cut)
        send1[t * cut : (t + 1) * cut] = total(at + (1 - place[2]) * cut).astype(BF16)


def put_rider(rider, dst, at):
    parts = []
    for _ in range(3):
        part = rider.astype(BF16)
        rider = rider - part.astype(F32)
        parts.append(part.astype(F32))
    parts.append(jnp.zeros((16 - 3 * rider.shape[0], rider.shape[1]), F32))
    dst[at : at + 16] = jnp.concatenate(parts, axis=0).astype(BF16)


def get_rider(src, at, n):
    rows = src[at : at + 16].astype(F32)
    return (rows[:n] + rows[n : 2 * n]) + rows[2 * n : 3 * n]


def middle_kernel(place, stay1_ref, recv1_ref, stay2_ref, b_ref, c_ref, a_ref, rider_ref, got_ref, *outs):
    stay1, sends, stay2, send2, rider_out = outs[0], outs[1:4], outs[4], outs[5], outs[6]
    rider = rider_ref[...] + got_ref[...]
    rider_out[...] = rider
    n = stay1.shape[0]

    def total(other):
        rows = pl.ds(pl.multiple_of(jnp.bitwise_xor(place[0], other) * n, 16), n)
        return stay1_ref[rows] + recv1_ref[rows].astype(F32)

    stay1[...] = total(0)
    for k, send in zip(OTHERS, sends):
        send[:n] = total(k).astype(BF16)
        put_rider(rider, send, n)
    m = stay2.shape[0]

    def summed(bit):
        rows = pl.ds(pl.multiple_of(bit * m, 16), m)
        first = stay2_ref[rows] + a_ref[rows].astype(F32)
        return first + (b_ref[rows].astype(F32) + c_ref[rows].astype(F32))

    stay2[...] = summed(place[2])
    send2[...] = summed(1 - place[2]).astype(BF16)


def last_kernel(stay1_ref, b_ref, c_ref, a_ref, stay2_ref, recv2_ref, rider_ref, o_ref, gain_ref, bias_ref):
    for k in range(stay2_ref.shape[0] // 16):
        two, one = slice(16 * k, 16 * k + 16), slice(32 * k, 32 * k + 32)
        near = stay1_ref[one] + a_ref[one].astype(F32)
        o_ref[48 * k : 48 * k + 32] = near + (b_ref[one].astype(F32) + c_ref[one].astype(F32))
        o_ref[48 * k + 32 : 48 * k + 48] = stay2_ref[two] + recv2_ref[two].astype(F32)
    n = stay1_ref.shape[0]
    near, b, c = (get_rider(ref, n, 2) for ref in (a_ref, b_ref, c_ref))
    rider = (rider_ref[...] + near) + (b + c)
    gain_ref[...] = rider[:1]
    bias_ref[...] = rider[1:]


def bits_of(axis):
    return [1 << k for k in range((lax.axis_size(axis) - 1).bit_length())]


def swap(value, axis, step):
    return lax.ppermute(value, axis, [(i, i ^ step) for i in range(lax.axis_size(axis))])


def together(*values):
    return lax.optimization_barrier(values)


def all_sum(value, axes):
    for axis in axes:
        for step in bits_of(axis):
            value = value + swap(value, axis, step)
    return value


def parted(value, axis, step):
    value = value.reshape((value.shape[0] // 2, 2) + value.shape[1:])
    bit = jnp.minimum(jnp.bitwise_and(lax.axis_index(axis), step), 1)
    keep = lax.dynamic_index_in_dim(value, bit, 1, keepdims=False)
    send = lax.dynamic_index_in_dim(value, 1 - bit, 1, keepdims=False)
    return keep, send.astype(BF16)


def body(clips, gain, bias, weight, cotangent):
    x, g = clips[0], cotangent[0]
    frames, rows, cols, chan_in = x.shape
    chan_out = g.shape[-1]
    per_group = chan_in // GROUPS
    tm, dp, width = (lax.axis_size(name) for name in ("tm", "dp", "width"))
    per_frame = float(rows * width * cols * per_group)
    z, core = lax.axis_index("tm"), lax.axis_index("width")
    place = jnp.stack([z, core, lax.axis_index("dp")]).astype(jnp.int32)
    cells = rows * cols
    shape = jax.ShapeDtypeStruct
    half = chan_out // 2

    up = [(i, i + 1) for i in range(tm - 1)]
    down = [(i + 1, i) for i in range(tm - 1)]
    affine = jnp.pad(jnp.stack([gain, bias]), ((0, 2 * frames - 2), (0, 0)))[None]
    x, g, place = together(x, g, place)
    g_first = g.reshape(frames, cells, chan_out)[:2]
    flat = x.reshape(frames, cells, chan_in)
    g_next = lax.ppermute(g_first, "tm", down).reshape(2, rows, cols, chan_out)
    sums, x_last, g_rows, x_rows, x_near, g_near = call(
        functools.partial(prepare_kernel, per_group),
        (
            shape((2 * frames, chan_in), F32),
            shape((2, rows, cols, chan_in), BF16),
            shape((frames, cols, chan_out), BF16),
            shape((frames, cols, chan_in), BF16),
            shape(x.shape, BF16),
            shape(g.shape, BF16),
        ),
        [place, far(x), far(g)],
        [pltpu.SemaphoreType.DMA((2 * frames,))],
        scalars=1,
        far=2,
    )
    sums = sums + swap(sums, "width", 1)
    g_edge = swap(g_rows, "width", 1)
    x_edge = swap(x_rows, "width", 1)
    x, g = x_near, g_near
    flat = x.reshape(frames, cells, chan_in)
    sums, g = together(sums, g)
    own_grad = call(
        own_grad_kernel,
        shape((frames, rows, cols, 3 * chan_in), F32),
        [g, weight],
        [pltpu.VMEM((frames, rows + 2, cols, chan_out), BF16)],
    )
    sums, g_next, g_edge, x_edge, own_grad = together(sums, g_next, g_edge, x_edge, own_grad)

    def edges(*values):
        rows_out = (sum(v.shape[0] for v in values), cols, values[0].shape[3])
        return call(edge_kernel, shape(rows_out, BF16), [place, *values], scalars=1)

    next_edge = swap(edges(g_next), "width", 1)
    stats = sums[None]
    for step in bits_of("tm"):
        stats = jnp.concatenate([stats, swap(stats, "tm", step)], axis=0)
    stats = jnp.concatenate([stats, affine], axis=0)
    stats, next_edge, x_last, x_rows = together(stats, next_edge, x_last, x_rows)
    x_prev = lax.ppermute(x_last, "tm", [(i, (i + 1) % tm) for i in range(tm)])
    turn = [(i * width + c, (i + 1) % tm * width + (c ^ 1)) for i in range(tm) for c in range(width)]
    prev_edge = lax.ppermute(x_rows[frames - 2 :], ("tm", "width"), turn)

    share = 27 * chan_in // (tm * dp)
    pieces = share % 48 == 0 and tm == 4 and dp == 2
    count = 3 * chan_in // 48
    if pieces:
        skip = chan_in
        late = lambda k: k // 3 if k % 3 == 2 else count + k // 3 * 2 + k % 3
    else:
        skip = 0
        late = lambda k: k
    keep, send = call(
        functools.partial(kernel_grad_kernel, per_frame, late, skip),
        (shape((27 * chan_in, half), F32), shape((27 * chan_in, half), BF16)),
        [place, stats, g_next, g_edge, next_edge, flat, g],
        [
            pltpu.VMEM((3 * chan_in, frames * cells), BF16),
            pltpu.VMEM((frames + 2, rows + 2, cols, chan_out), BF16),
        ],
        scalars=1,
    )
    send, x_prev, prev_edge, hold = together(send, x_prev, prev_edge, stats)
    recv = swap(send, "width", 1)
    local = call(
        functools.partial(gain_kernel, per_frame),
        shape((2, chan_in), F32),
        [place, hold, flat, own_grad, g_next, g_edge, next_edge, weight],
        [
            pltpu.VMEM((2, rows + 2, cols, chan_out), BF16),
            pltpu.VMEM((frames, rows, cols, 3 * chan_in), F32),
        ],
        scalars=1,
    )
    recv, local = together(recv, local)

    def outputs(hold):
        return call(
            functools.partial(output_kernel, per_frame),
            shape((frames * cells, chan_out), BF16),
            [place, hold, x, x_prev, x_edge, prev_edge, weight],
            [
                pltpu.VMEM((frames + 2, rows + 2, cols, 3 * chan_in), BF16),
                pltpu.VMEM((frames * cells, chan_out), F32),
            ],
            scalars=1,
        )

    if not pieces:
        output = outputs(stats)
        one = keep + recv.astype(F32)
        one = jnp.moveaxis(one.reshape(tm, dp, share, half), 1, 0)
        for step in bits_of("dp"):
            one, send = parted(one, "dp", step)
            one = one + swap(send, "dp", step).astype(F32)
        one = one[0]
        for step in bits_of("tm"):
            one, send = parted(one, "tm", step)
            one = one + swap(send, "tm", step).astype(F32)
        rider = all_sum(local, ("width", "dp", "tm"))
        grad_weight = one[0]
    else:
        rest = share // 3
        cut = share - rest

        def piece(n, kind):
            return shape((n, half), kind)

        both = dp * rest
        stay1, send1, stay2, *send2 = call(
            functools.partial(split_kernel, cut, both),
            [piece(tm * cut, F32), piece(tm * cut, BF16), piece(both, F32)] + [piece(both, BF16)] * (tm - 1),
            [place, keep, recv],
            scalars=1,
        )
        rider = local + swap(local, "width", 1)
        send1, hold, rider, *send2 = together(send1, hold, rider, *send2)
        recv1 = swap(send1, "dp", 1)
        recv2 = [swap(v, "tm", k) for k, v in zip(OTHERS, send2)]
        got = swap(rider, "dp", 1)
        recv1, got, *recv2 = together(recv1, got, *recv2)
        stay1, *send1, stay2, send2, rider = call(
            middle_kernel,
            [piece(cut, F32)]
            + [piece(cut + 16, BF16)] * (tm - 1)
            + [piece(rest, F32), piece(rest, BF16), shape(rider.shape, F32)],
            [place, stay1, recv1, stay2, *recv2, rider, got],
            scalars=1,
        )
        send2, hold, *send1 = together(send2, hold, *send1)
        recv1 = [swap(v, "tm", k) for k, v in zip(OTHERS, send1)]
        recv2 = swap(send2, "dp", 1)
        output = outputs(hold)
        recv2, output, *recv1 = together(recv2, output, *recv1)
        row = shape((1, chan_in), F32)
        grad_weight, *rider = call(
            last_kernel, [piece(share, F32), row, row], [stay1, *recv1, stay2, recv2, rider]
        )
        rider = [v.reshape(chan_in) for v in rider]
    return (output.reshape(1, frames, rows, cols, chan_out), grad_weight, rider[0], rider[1])


def solution(mesh):
    return jax.shard_map(
        body,
        mesh=mesh,
        in_specs=(
            P(("groups", "dp"), "tm", "width", None, None),
            P(),
            P(),
            P(),
            P(("groups", "dp"), "tm", "width", None, None),
        ),
        out_specs=(
            P(("groups", "dp"), "tm", "width", None, None),
            P(("groups", "tm", "dp"), "width"),
            P("groups"),
            P("groups"),
        ),
        check_vma=False,
    )
```

```python
import functools

import jax
import jax.numpy as jnp
from jax import lax
from jax.experimental import pallas as pl
from jax.experimental.pallas import tpu as pltpu
from jax.sharding import PartitionSpec as P

GROUPS = 32
OTHERS = (2, 3, 1)
F32, BF16 = jnp.float32, jnp.bfloat16
VMEM = pl.BlockSpec(memory_space=pltpu.VMEM)
SMEM = pl.BlockSpec(memory_space=pltpu.SMEM)
HBM = pl.BlockSpec(memory_space=pltpu.HBM)


def call(kernel, out_shape, inputs, scratch=(), flops=0, scalars=0, far=0):
    outs = jax.tree.leaves(out_shape)
    moved = sum(v.size * v.dtype.itemsize for v in list(inputs) + list(outs))
    return pl.pallas_call(
        kernel,
        out_shape=out_shape,
        in_specs=[SMEM] * scalars + [VMEM] * (len(inputs) - scalars - far) + [HBM] * far,
        out_specs=jax.tree.map(lambda _: VMEM, out_shape),
        scratch_shapes=list(scratch),
        cost_estimate=pl.CostEstimate(flops=0, bytes_accessed=moved, transcendentals=0),
        compiler_params=pltpu.CompilerParams(vmem_limit_bytes=16 << 20),
    )(*inputs)


def far(value):
    return pltpu.with_memory_space_constraint(value, pltpu.HBM)


def group_sum(rows, per_group):
    lane = lax.broadcasted_iota(jnp.int32, rows.shape, 1)
    lanes = rows.shape[1]
    step = 1
    while step < per_group:
        up = pltpu.roll(rows, lanes - step, 1)
        down = pltpu.roll(rows, step, 1)
        rows = rows + jnp.where((lane // step) % 2 == 0, up, down)
        step *= 2
    return rows


def prepare_kernel(per_group, place, x_hbm, g_hbm, sums_ref, odd_ref, even_ref, row_ref, x_row_ref, x_ref, g_ref, sems):
    frames, rows, cols, chan_in = x_ref.shape
    row = jnp.where(place[1] == 0, rows - 1, 0)
    copies = [pltpu.make_async_copy(x_hbm.at[t], x_ref.at[t], sems.at[t]) for t in range(frames)]
    copies += [pltpu.make_async_copy(g_hbm.at[t], g_ref.at[t], sems.at[frames + t]) for t in range(frames)]
    for copy in copies:
        copy.start()
    firsts, squares = [], []
    for t in range(frames):
        copies[t].wait()
        v = x_ref[t].reshape(rows * cols, chan_in).astype(F32)
        firsts.append(jnp.sum(v, axis=0, keepdims=True))
        squares.append(jnp.sum(v * v, axis=0, keepdims=True))
        x_row_ref[t] = x_ref[t, row]
    sums_ref[...] = group_sum(jnp.concatenate(firsts + squares, axis=0), per_group)
    for t in range(frames):
        copies[frames + t].wait()
        row_ref[t] = g_ref[t, row]
    even = jnp.bitwise_and(place[0], 1) == 0
    for t in range(2):
        clip, low = x_ref[frames - 2 + t], g_ref[t, :, :, :chan_in]
        odd_ref[t, :, :, :chan_in] = jnp.where(even, clip, low)
        even_ref[t, :, :, :chan_in] = jnp.where(even, low, clip)
        odd_ref[t, :, :, chan_in:] = g_ref[t, :, :, chan_in:]
        even_ref[t, :, :, chan_in:] = g_ref[t, :, :, chan_in:]


def arrived_kernel(place, odd_ref, even_ref, next_ref, prev_ref, edge_ref):
    chan_in, chan_out = prev_ref.shape[3], next_ref.shape[3]
    even = jnp.bitwise_and(place[0], 1) == 0
    row = jnp.where(place[1] == 0, next_ref.shape[1] - 1, 0)
    for t in range(2):
        next_ref[t] = jnp.where(even, odd_ref[t], even_ref[t])
        prev_ref[t] = jnp.where(even, even_ref[t, :, :, :chan_in], odd_ref[t, :, :, :chan_in])
        edge_ref[t, :, :chan_out] = next_ref[t, row]
        edge_ref[t, :, chan_out:] = prev_ref[t, row]


def frame_stats(place, stats_ref, frames, per_frame):
    devices = stats_ref.shape[0] - 1
    mine = place[0]
    own = stats_ref[0]
    before = jnp.zeros_like(own)
    behind = jnp.zeros_like(own)
    for x in range(1, devices):
        other = jnp.bitwise_xor(mine, x)
        rows = stats_ref[x]
        before = before + jnp.where(other < mine - 1, rows, 0.0)
        behind = behind + jnp.where(other == mine - 1, rows, 0.0)

    def total(rows, at):
        return jnp.sum(rows[at : at + frames], axis=0, keepdims=True)

    first, square = total(before, 0), total(before, frames)
    means, inverses = [], []
    for k in range(2 * frames):
        rows, t = (behind, k) if k < frames else (own, k - frames)
        first = first + rows[t : t + 1]
        square = square + rows[frames + t : frames + t + 1]
        if k < frames - 2:
            continue
        shown = jnp.maximum(mine * frames + k - frames + 1, 1).astype(F32) * per_frame
        mean = first / shown
        variance = square / shown - mean * mean
        means.append(mean)
        inverses.append(lax.rsqrt(variance + 1e-05))
    return means, inverses


def pad_rows(core, own, edge, dst):
    rows = own.shape[1]
    zero = jnp.zeros_like(edge)
    dst[:, 0] = jnp.where(core == 0, zero, edge)
    dst[:, rows + 1] = jnp.where(core == 0, edge, zero)
    dst[:, 1 : rows + 1] = own


def by_taps(window, w_ref, tap, chan_in):
    size = 3 * chan_in
    start = tap * size if isinstance(tap, int) else pl.multiple_of(tap * size, size)
    return lax.dot_general(
        window, w_ref[pl.ds(start, size)], (((1,), (1,)), ((), ())), preferred_element_type=F32
    )


def own_grad_kernel(g_ref, w_ref, z_ref, gp_ref):
    frames, rows, cols, chan_out = g_ref.shape
    chan_in = z_ref.shape[3] // 3
    zero = jnp.zeros((frames, cols, chan_out), BF16)
    gp_ref[:, 0] = zero
    gp_ref[:, rows + 1] = zero
    gp_ref[:, 1 : rows + 1] = g_ref[...]
    for a in (2, 1, 0):
        n = frames - 2 + a
        for b in range(3):
            window = gp_ref[2 - a :, 2 - b : 2 - b + rows].reshape(n * rows * cols, chan_out)
            part = by_taps(window, w_ref, a * 3 + b, chan_in).reshape(n, rows, cols, 3 * chan_in)
            if a == 2 and b == 0:
                z_ref[...] = part
            else:
                z_ref[:n] += part


def gain_kernel(
    per_frame, place, stats_ref, x_ref, own_ref, next_ref, edge_ref, edge_next, w_ref, o_ref, gp_ref, z_ref
):
    frames, rows, cols, chan_out = own_ref.shape[:3] + (next_ref.shape[3],)
    chan_in = x_ref.shape[2]
    cells = rows * cols
    core = place[1]
    pad_rows(core, next_ref[...], edge_next[:, :, :chan_out], gp_ref)
    z_ref[...] = own_ref[...]
    for a in range(2):
        n = 2 - a
        for b in range(3):
            window = gp_ref[:n, 2 - b : 2 - b + rows].reshape(n * cells, chan_out)
            part = by_taps(window, w_ref, a * 3 + b, chan_in).reshape(n, rows, cols, 3 * chan_in)
            z_ref[frames - n :] += part
    row = jnp.where(core == 0, rows - 1, 0)
    tap_row = jnp.where(core == 0, 0, 2)
    for a in range(3):
        n = frames - 2 + a
        window = edge_ref[2 - a : frames].reshape(n * cols, chan_out)
        part = by_taps(window, w_ref, a * 3 + tap_row, chan_in)
        for t in range(n):
            z_ref[t, row] += part[t * cols : (t + 1) * cols]
    means, inverses = frame_stats(place, stats_ref, frames, per_frame)
    affine = stats_ref[stats_ref.shape[0] - 1]
    gain, bias = affine[:1], affine[1:2]
    col = lax.broadcasted_iota(jnp.int32, (cells, chan_in), 0) % cols
    by_gain = jnp.zeros((1, chan_in), F32)
    by_bias = jnp.zeros((1, chan_in), F32)
    for t in range(frames):
        z = z_ref[t].reshape(cells, 3 * chan_in)
        left = jnp.where(col == cols - 1, 0.0, pltpu.roll(z[:, :chan_in], cells - 1, 0))
        right = jnp.where(col == 0, 0.0, pltpu.roll(z[:, 2 * chan_in :], 1, 0))
        grad_hidden = left + z[:, chan_in : 2 * chan_in] + right
        normed = (x_ref[t].astype(F32) - means[2 + t]) * inverses[2 + t]
        act = normed * gain + bias
        sigma = lax.logistic(act)
        grad_act = grad_hidden * sigma * (1.0 + act * (1.0 - sigma))
        by_gain = by_gain + jnp.sum(grad_act * normed, axis=0, keepdims=True)
        by_bias = by_bias + jnp.sum(grad_act, axis=0, keepdims=True)
    o_ref[...] = jnp.concatenate([by_gain, by_bias], axis=0)


def kernel_grad_kernel(
    per_frame, late, skip, place, stats_ref, next_ref, edge_ref, edge_next, x_ref, g_ref, *rest
):
    keep_ref, send_ref, ht_ref, gp_ref = rest
    frames, cells, chan_in = x_ref.shape
    rows, cols, chan_out = g_ref.shape[1:]
    core = place[1]
    pad_rows(core, g_ref[...], edge_ref[...], gp_ref.at[:frames])
    pad_rows(core, next_ref[...], edge_next[:, :, :chan_out], gp_ref.at[frames:])
    means, inverses = frame_stats(place, stats_ref, frames, per_frame)
    affine = stats_ref[stats_ref.shape[0] - 1]
    gain, bias = affine[:1], affine[1:2]
    block = 2 * cols
    lane = lax.broadcasted_iota(jnp.int32, (chan_in, block), 1) % cols
    for t in range(frames):
        for half in range(cells // block):
            v = x_ref[t, half * block : (half + 1) * block].astype(F32)
            act = (v - means[2 + t]) * inverses[2 + t] * gain + bias
            hidden = (act * lax.logistic(act)).astype(BF16).astype(F32)
            turned = hidden.T
            at = t * cells + half * block
            earlier = jnp.where(lane == 0, 0.0, pltpu.roll(turned, 1, 1))
            later = jnp.where(lane == cols - 1, 0.0, pltpu.roll(turned, block - 1, 1))
            for d, piece in enumerate((earlier, turned, later)):
                piece = piece.astype(BF16)
                for k in range(chan_in // 16):
                    to = late(d * (chan_in // 16) + k) * 16
                    ht_ref[to : to + 16, at : at + block] = piece[k * 16 : (k + 1) * 16]
    mine = chan_out // 2
    n = 3 * chan_in
    for a in range(3):
        for b in range(3):
            tap = a * 3 + b
            window = gp_ref[2 - a : 2 - a + frames, 2 - b : 2 - b + rows].reshape(frames * cells, chan_out)
            part = jnp.dot(ht_ref[...], window, preferred_element_type=F32)
            low, high = part[:, :mine], part[:, mine:]
            keep = jnp.where(core == 0, low, high)
            send = jnp.where(core == 0, high, low).astype(BF16)
            for begin, end, at in ((0, skip, tap * skip), (skip, n, 9 * skip + tap * (n - skip))):
                if end > begin:
                    keep_ref[at : at + end - begin] = keep[begin:end]
                    send_ref[at : at + end - begin] = send[begin:end]


def hidden_kernel(
    per_frame, place, stats_ref, x_ref, prev_ref, edge_ref, prev_edge, h_ref
):
    frames, rows, cols, chan_in = x_ref.shape
    mine, core = place[0], place[1]
    means, inverses = frame_stats(place, stats_ref, frames, per_frame)
    affine = stats_ref[stats_ref.shape[0] - 1]
    gain, bias = affine[:1], affine[1:2]

    def put(f, r0, rows_now, value, keep):
        act = (value.astype(F32) - means[f]) * inverses[f] * gain + bias
        hidden = act * lax.logistic(act)
        if keep is not None:
            hidden = jnp.where(keep, hidden, 0.0)
        n = rows_now * cols
        col = lax.broadcasted_iota(jnp.int32, (n, chan_in), 0) % cols
        earlier = jnp.where(col == 0, 0.0, pltpu.roll(hidden, 1, 0))
        later = jnp.where(col == cols - 1, 0.0, pltpu.roll(hidden, n - 1, 0))
        for d, piece in enumerate((earlier, hidden, later)):
            h_ref[f, r0 : r0 + rows_now, :, d * chan_in : (d + 1) * chan_in] = piece.astype(BF16).reshape(
                rows_now, cols, chan_in
            )

    for f in range(frames + 2):
        inside = (mine > 0) if f < 2 else None
        value = prev_ref[f] if f < 2 else x_ref[f - 2]
        put(f, 1, rows, value.reshape(rows * cols, chan_in), inside)
        for r0, here in ((0, core == 1), (rows + 1, core == 0)):
            put(f, r0, 1, prev_edge[f, :, prev_edge.shape[2] - chan_in :] if f < 2 else edge_ref[f - 2], here if inside is None else jnp.logical_and(here, inside))


def output_kernel(h_ref, w_ref, o_ref, acc_ref):
    frames, rows, cols, size = h_ref.shape
    frames, rows = frames - 2, rows - 2
    cells = frames * rows * cols
    for a in range(3):
        for b in range(3):
            tap = a * 3 + b
            window = h_ref[a : a + frames, b : b + rows].reshape(cells, size)
            part = jnp.dot(window, w_ref[tap * size : (tap + 1) * size], preferred_element_type=F32)
            if tap == 0:
                acc_ref[...] = part
            elif tap < 8:
                acc_ref[...] += part
            else:
                o_ref[...] = (acc_ref[...] + part).astype(BF16)


def split_kernel(cut, rest, place, keep_ref, recv_ref, stay1, send1, stay2, *send2):
    tm = len(send2) + 1

    def total(at):
        rows = pl.ds(pl.multiple_of(at, 16), size)
        return keep_ref[rows] + recv_ref[rows].astype(F32)

    size = rest
    stay2[...] = total(place[0] * rest)
    for k, send in zip(OTHERS, send2):
        send[...] = total(jnp.bitwise_xor(place[0], k) * rest).astype(BF16)
    size = cut
    for t in range(tm):
        at = tm * rest + 2 * t * cut
        stay1[t * cut : (t + 1) * cut] = total(at + place[2] * cut)
        send1[t * cut : (t + 1) * cut] = total(at + (1 - place[2]) * cut).astype(BF16)


def put_rider(rider, dst, at):
    parts = []
    for _ in range(3):
        part = rider.astype(BF16)
        rider = rider - part.astype(F32)
        parts.append(part.astype(F32))
    parts.append(jnp.zeros((16 - 3 * rider.shape[0], rider.shape[1]), F32))
    dst[at : at + 16] = jnp.concatenate(parts, axis=0).astype(BF16)


def get_rider(src, at, n):
    rows = src[at : at + 16].astype(F32)
    return (rows[:n] + rows[n : 2 * n]) + rows[2 * n : 3 * n]


def middle_kernel(place, stay1_ref, recv1_ref, stay2_ref, b_ref, c_ref, a_ref, rider_ref, got_ref, *outs):
    stay1, sends, stay2, send2, rider_out = outs[0], outs[1:4], outs[4], outs[5], outs[6]
    rider = rider_ref[...] + got_ref[...]
    rider_out[...] = rider
    n = stay1.shape[0]

    def total(other):
        rows = pl.ds(pl.multiple_of(jnp.bitwise_xor(place[0], other) * n, 16), n)
        return stay1_ref[rows] + recv1_ref[rows].astype(F32)

    stay1[...] = total(0)
    for k, send in zip(OTHERS, sends):
        send[:n] = total(k).astype(BF16)
        put_rider(rider, send, n)
    m = stay2.shape[0]

    def summed(bit):
        rows = pl.ds(pl.multiple_of(bit * m, 16), m)
        first = stay2_ref[rows] + a_ref[rows].astype(F32)
        return first + (b_ref[rows].astype(F32) + c_ref[rows].astype(F32))

    stay2[...] = summed(place[2])
    send2[...] = summed(1 - place[2]).astype(BF16)


def last_kernel(stay1_ref, b_ref, c_ref, a_ref, stay2_ref, recv2_ref, rider_ref, o_ref, gain_ref, bias_ref):
    for k in range(stay2_ref.shape[0] // 16):
        two, one = slice(16 * k, 16 * k + 16), slice(32 * k, 32 * k + 32)
        near = stay1_ref[one] + a_ref[one].astype(F32)
        o_ref[48 * k : 48 * k + 32] = near + (b_ref[one].astype(F32) + c_ref[one].astype(F32))
        o_ref[48 * k + 32 : 48 * k + 48] = stay2_ref[two] + recv2_ref[two].astype(F32)
    n = stay1_ref.shape[0]
    near, b, c = (get_rider(ref, n, 2) for ref in (a_ref, b_ref, c_ref))
    rider = (rider_ref[...] + near) + (b + c)
    gain_ref[...] = rider[:1]
    bias_ref[...] = rider[1:]


def bits_of(axis):
    return [1 << k for k in range((lax.axis_size(axis) - 1).bit_length())]


def swap(value, axis, step):
    return lax.ppermute(value, axis, [(i, i ^ step) for i in range(lax.axis_size(axis))])


def together(*values):
    return lax.optimization_barrier(values)


def all_sum(value, axes):
    for axis in axes:
        for step in bits_of(axis):
            value = value + swap(value, axis, step)
    return value


def parted(value, axis, step):
    value = value.reshape((value.shape[0] // 2, 2) + value.shape[1:])
    bit = jnp.minimum(jnp.bitwise_and(lax.axis_index(axis), step), 1)
    keep = lax.dynamic_index_in_dim(value, bit, 1, keepdims=False)
    send = lax.dynamic_index_in_dim(value, 1 - bit, 1, keepdims=False)
    return keep, send.astype(BF16)


def body(clips, gain, bias, weight, cotangent):
    x, g = clips[0], cotangent[0]
    frames, rows, cols, chan_in = x.shape
    chan_out = g.shape[-1]
    per_group = chan_in // GROUPS
    tm, dp, width = (lax.axis_size(name) for name in ("tm", "dp", "width"))
    per_frame = float(rows * width * cols * per_group)
    z, core = lax.axis_index("tm"), lax.axis_index("width")
    place = jnp.stack([z, core, lax.axis_index("dp")]).astype(jnp.int32)
    cells = rows * cols
    shape = jax.ShapeDtypeStruct
    half = chan_out // 2

    odd_pairs = [(i, i ^ 1) for i in range(tm)]
    even_pairs = [(i, i + 1 if i % 2 else i - 1) for i in range(1, tm - 1)]
    affine = jnp.pad(jnp.stack([gain, bias]), ((0, 2 * frames - 2), (0, 0)))[None]
    x, g, place = together(x, g, place)
    sums, to_odd, to_even, g_rows, x_rows, x_near, g_near = call(
        functools.partial(prepare_kernel, per_group),
        (
            shape((2 * frames, chan_in), F32),
            shape((2, rows, cols, chan_out), BF16),
            shape((2, rows, cols, chan_out), BF16),
            shape((frames, cols, chan_out), BF16),
            shape((frames, cols, chan_in), BF16),
            shape(x.shape, BF16),
            shape(g.shape, BF16),
        ),
        [place, far(x), far(g)],
        [pltpu.SemaphoreType.DMA((2 * frames,))],
        scalars=1,
        far=2,
    )
    from_odd = lax.ppermute(to_odd, "tm", odd_pairs)
    from_even = lax.ppermute(to_even, "tm", even_pairs)
    sums = sums + swap(sums, "width", 1)
    g_edge = swap(g_rows, "width", 1)
    x_edge = swap(x_rows, "width", 1)
    x, g = x_near, g_near
    flat = x.reshape(frames, cells, chan_in)
    sums, g = together(sums, g)
    own_grad = call(
        own_grad_kernel,
        shape((frames, rows, cols, 3 * chan_in), F32),
        [g, weight],
        [pltpu.VMEM((frames, rows + 2, cols, chan_out), BF16)],
    )
    sums, from_odd, from_even, g_edge, x_edge, own_grad = together(sums, from_odd, from_even, g_edge, x_edge, own_grad)

    g_next, x_prev, next_edge = call(
        arrived_kernel,
        (
            shape((2, rows, cols, chan_out), BF16),
            shape((2, rows, cols, chan_in), BF16),
            shape((2, cols, chan_out + chan_in), BF16),
        ),
        [place, from_odd, from_even],
        scalars=1,
    )
    next_edge = swap(next_edge, "width", 1)
    if tm <= 4:
        found = [sums] + [swap(sums, "tm", k) for k in range(1, tm)]
        stats = jnp.stack(found)
    else:
        stats = sums[None]
        for step in bits_of("tm"):
            stats = jnp.concatenate([stats, swap(stats, "tm", step)], axis=0)
    stats = jnp.concatenate([stats, affine], axis=0)
    stats, next_edge, x_prev = together(stats, next_edge, x_prev)

    share = 27 * chan_in // (tm * dp)
    pieces = share % 48 == 0 and tm == 4 and dp == 2
    count = 3 * chan_in // 48
    if pieces:
        skip = chan_in
        late = lambda k: k // 3 if k % 3 == 2 else count + k // 3 * 2 + k % 3
    else:
        skip = 0
        late = lambda k: k
    keep, send = call(
        functools.partial(kernel_grad_kernel, per_frame, late, skip),
        (shape((27 * chan_in, half), F32), shape((27 * chan_in, half), BF16)),
        [place, stats, g_next, g_edge, next_edge, flat, g],
        [
            pltpu.VMEM((3 * chan_in, frames * cells), BF16),
            pltpu.VMEM((frames + 2, rows + 2, cols, chan_out), BF16),
        ],
        scalars=1,
    )
    send, hold = together(send, stats)
    recv = swap(send, "width", 1)
    local = call(
        functools.partial(gain_kernel, per_frame),
        shape((2, chan_in), F32),
        [place, hold, flat, own_grad, g_next, g_edge, next_edge, weight],
        [
            pltpu.VMEM((2, rows + 2, cols, chan_out), BF16),
            pltpu.VMEM((frames, rows, cols, 3 * chan_in), F32),
        ],
        scalars=1,
    )
    recv, local = together(recv, local)

    def activations(hold):
        return call(
            functools.partial(hidden_kernel, per_frame),
            shape((frames + 2, rows + 2, cols, 3 * chan_in), BF16),
            [place, hold, x, x_prev, x_edge, next_edge],
            scalars=1,
        )

    def outputs(hidden):
        return call(
            output_kernel,
            shape((frames * cells, chan_out), BF16),
            [hidden, weight],
            [pltpu.VMEM((frames * cells, chan_out), F32)],
        )

    if not pieces:
        output = outputs(activations(stats))
        one = keep + recv.astype(F32)
        one = jnp.moveaxis(one.reshape(tm, dp, share, half), 1, 0)
        for step in bits_of("dp"):
            one, send = parted(one, "dp", step)
            one = one + swap(send, "dp", step).astype(F32)
        one = one[0]
        for step in bits_of("tm"):
            one, send = parted(one, "tm", step)
            one = one + swap(send, "tm", step).astype(F32)
        rider = all_sum(local, ("width", "dp", "tm"))
        grad_weight = one[0]
    else:
        rest = share // 3
        cut = share - rest

        def piece(n, kind):
            return shape((n, half), kind)

        both = dp * rest
        stay1, send1, stay2, *send2 = call(
            functools.partial(split_kernel, cut, both),
            [piece(tm * cut, F32), piece(tm * cut, BF16), piece(both, F32)] + [piece(both, BF16)] * (tm - 1),
            [place, keep, recv],
            scalars=1,
        )
        rider = local + swap(local, "width", 1)
        send1, hold, rider, *send2 = together(send1, hold, rider, *send2)
        recv2 = [swap(send2[0], "tm", OTHERS[0])]
        recv1 = swap(send1, "dp", 1)
        recv2 += [swap(v, "tm", k) for k, v in zip(OTHERS[1:], send2[1:])]
        got = swap(rider, "dp", 1)
        recv1, got, hidden, *recv2 = together(recv1, got, activations(hold), *recv2)
        stay1, *send1, stay2, send2, rider = call(
            middle_kernel,
            [piece(cut, F32)]
            + [piece(cut + 16, BF16)] * (tm - 1)
            + [piece(rest, F32), piece(rest, BF16), shape(rider.shape, F32)],
            [place, stay1, recv1, stay2, *recv2, rider, got],
            scalars=1,
        )
        send2, hidden, *send1 = together(send2, hidden, *send1)
        recv1 = [swap(v, "tm", k) for k, v in zip(OTHERS, send1)]
        recv2 = swap(send2, "dp", 1)
        output = outputs(hidden)
        recv2, output, *recv1 = together(recv2, output, *recv1)
        row = shape((1, chan_in), F32)
        grad_weight, *rider = call(
            last_kernel, [piece(share, F32), row, row], [stay1, *recv1, stay2, recv2, rider]
        )
        rider = [v.reshape(chan_in) for v in rider]
    return (output.reshape(1, frames, rows, cols, chan_out), grad_weight, rider[0], rider[1])


def solution(mesh):
    return jax.shard_map(
        body,
        mesh=mesh,
        in_specs=(
            P(("groups", "dp"), "tm", "width", None, None),
            P(),
            P(),
            P(),
            P(("groups", "dp"), "tm", "width", None, None),
        ),
        out_specs=(
            P(("groups", "dp"), "tm", "width", None, None),
            P(("groups", "tm", "dp"), "width"),
            P("groups"),
            P("groups"),
        ),
        check_vma=False,
    )
```

```python
import functools

import jax
import jax.numpy as jnp
from jax import lax
from jax.experimental import pallas as pl
from jax.experimental.pallas import tpu as pltpu
from jax.sharding import PartitionSpec as P

GROUPS = 32
OTHERS = (2, 3, 1)
F32, BF16 = jnp.float32, jnp.bfloat16
VMEM = pl.BlockSpec(memory_space=pltpu.VMEM)
SMEM = pl.BlockSpec(memory_space=pltpu.SMEM)
HBM = pl.BlockSpec(memory_space=pltpu.HBM)


def call(kernel, out_shape, inputs, scratch=(), flops=0, scalars=0, far=0):
    outs = jax.tree.leaves(out_shape)
    moved = sum(v.size * v.dtype.itemsize for v in list(inputs) + list(outs))
    return pl.pallas_call(
        kernel,
        out_shape=out_shape,
        in_specs=[SMEM] * scalars + [VMEM] * (len(inputs) - scalars - far) + [HBM] * far,
        out_specs=jax.tree.map(lambda _: VMEM, out_shape),
        scratch_shapes=list(scratch),
        cost_estimate=pl.CostEstimate(flops=0, bytes_accessed=moved, transcendentals=0),
        compiler_params=pltpu.CompilerParams(vmem_limit_bytes=16 << 20),
    )(*inputs)


def far(value):
    return pltpu.with_memory_space_constraint(value, pltpu.HBM)


def group_sum(rows, per_group):
    lane = lax.broadcasted_iota(jnp.int32, rows.shape, 1)
    lanes = rows.shape[1]
    step = 1
    while step < per_group:
        up = pltpu.roll(rows, lanes - step, 1)
        down = pltpu.roll(rows, step, 1)
        rows = rows + jnp.where((lane // step) % 2 == 0, up, down)
        step *= 2
    return rows


def prepare_kernel(per_group, place, x_hbm, g_hbm, sums_ref, odd_ref, even_ref, row_ref, x_row_ref, x_ref, g_ref, sems):
    frames, rows, cols, chan_in = x_ref.shape
    row = jnp.where(place[1] == 0, rows - 1, 0)
    copies = [pltpu.make_async_copy(x_hbm.at[t], x_ref.at[t], sems.at[t]) for t in range(frames)]
    copies += [pltpu.make_async_copy(g_hbm.at[t], g_ref.at[t], sems.at[frames + t]) for t in range(frames)]
    for copy in copies:
        copy.start()
    firsts, squares = [], []
    for t in range(frames):
        copies[t].wait()
        v = x_ref[t].reshape(rows * cols, chan_in).astype(F32)
        firsts.append(jnp.sum(v, axis=0, keepdims=True))
        squares.append(jnp.sum(v * v, axis=0, keepdims=True))
        x_row_ref[t] = x_ref[t, row]
    total = group_sum(jnp.concatenate(firsts + squares, axis=0), per_group)
    sums_ref[...] = total
    parts = []
    for _ in range(3):
        parts.append(total.astype(BF16).astype(F32))
        total = total - parts[-1]
    n = rows * cols
    odd_ref[2 * n :, :chan_in] = jnp.concatenate(parts[:2], axis=0).astype(BF16)
    odd_ref[2 * n :, chan_in:] = jnp.concatenate([parts[2], jnp.zeros_like(total)], axis=0).astype(BF16)
    for t in range(frames):
        copies[frames + t].wait()
        row_ref[t] = g_ref[t, row]
    even = jnp.bitwise_and(place[0], 1) == 0
    for t in range(2):
        clip, low = x_ref[frames - 2 + t], g_ref[t, :, :, :chan_in]
        here = slice(t * n, (t + 1) * n)
        odd_ref[here, :chan_in] = jnp.where(even, clip, low).reshape(n, chan_in)
        even_ref[t, :, :, :chan_in] = jnp.where(even, low, clip)
        odd_ref[here, chan_in:] = g_ref[t, :, :, chan_in:].reshape(n, chan_in)
        even_ref[t, :, :, chan_in:] = g_ref[t, :, :, chan_in:]


def arrived_kernel(place, odd_ref, even_ref, next_ref, prev_ref, edge_ref):
    chan_in, chan_out = prev_ref.shape[3], next_ref.shape[3]
    even = jnp.bitwise_and(place[0], 1) == 0
    row = jnp.where(place[1] == 0, next_ref.shape[1] - 1, 0)
    n = next_ref.shape[1] * next_ref.shape[2]
    for t in range(2):
        odd = odd_ref[t * n : (t + 1) * n].reshape(next_ref.shape[1:])
        next_ref[t] = jnp.where(even, odd, even_ref[t])
        prev_ref[t] = jnp.where(even, even_ref[t, :, :, :chan_in], odd[:, :, :chan_in])
        edge_ref[t, :, :chan_out] = next_ref[t, row]
        edge_ref[t, :, chan_out:] = prev_ref[t, row]


def frame_stats(place, stats_ref, frames, per_frame):
    devices = stats_ref.shape[0] - 1
    mine = place[0]
    own = stats_ref[0]
    before = jnp.zeros_like(own)
    behind = jnp.zeros_like(own)
    for x in range(1, devices):
        other = jnp.bitwise_xor(mine, x)
        rows = stats_ref[x]
        before = before + jnp.where(other < mine - 1, rows, 0.0)
        behind = behind + jnp.where(other == mine - 1, rows, 0.0)

    def total(rows, at):
        return jnp.sum(rows[at : at + frames], axis=0, keepdims=True)

    first, square = total(before, 0), total(before, frames)
    means, inverses = [], []
    for k in range(2 * frames):
        rows, t = (behind, k) if k < frames else (own, k - frames)
        first = first + rows[t : t + 1]
        square = square + rows[frames + t : frames + t + 1]
        if k < frames - 2:
            continue
        shown = jnp.maximum(mine * frames + k - frames + 1, 1).astype(F32) * per_frame
        mean = first / shown
        variance = square / shown - mean * mean
        means.append(mean)
        inverses.append(lax.rsqrt(variance + 1e-05))
    return means, inverses


def pad_rows(core, own, edge, dst):
    rows = own.shape[1]
    zero = jnp.zeros_like(edge)
    dst[:, 0] = jnp.where(core == 0, zero, edge)
    dst[:, rows + 1] = jnp.where(core == 0, edge, zero)
    dst[:, 1 : rows + 1] = own


def by_taps(window, w_ref, tap, chan_in):
    size = 3 * chan_in
    start = tap * size if isinstance(tap, int) else pl.multiple_of(tap * size, size)
    return lax.dot_general(
        window, w_ref[pl.ds(start, size)], (((1,), (1,)), ((), ())), preferred_element_type=F32
    )


def own_grad_kernel(g_ref, w_ref, z_ref, gp_ref):
    frames, rows, cols, chan_out = g_ref.shape
    chan_in = z_ref.shape[3] // 3
    zero = jnp.zeros((frames, cols, chan_out), BF16)
    gp_ref[:, 0] = zero
    gp_ref[:, rows + 1] = zero
    gp_ref[:, 1 : rows + 1] = g_ref[...]
    for a in (2, 1, 0):
        n = frames - 2 + a
        for b in range(3):
            window = gp_ref[2 - a :, 2 - b : 2 - b + rows].reshape(n * rows * cols, chan_out)
            part = by_taps(window, w_ref, a * 3 + b, chan_in).reshape(n, rows, cols, 3 * chan_in)
            if a == 2 and b == 0:
                z_ref[...] = part
            else:
                z_ref[:n] += part


def gain_kernel(
    per_frame, place, stats_ref, x_ref, own_ref, next_ref, edge_ref, edge_next, w_ref, o_ref, gp_ref, z_ref
):
    frames, rows, cols, chan_out = own_ref.shape[:3] + (next_ref.shape[3],)
    chan_in = x_ref.shape[2]
    cells = rows * cols
    core = place[1]
    pad_rows(core, next_ref[...], edge_next[:, :, :chan_out], gp_ref)
    z_ref[...] = own_ref[...]
    for a in range(2):
        n = 2 - a
        for b in range(3):
            window = gp_ref[:n, 2 - b : 2 - b + rows].reshape(n * cells, chan_out)
            part = by_taps(window, w_ref, a * 3 + b, chan_in).reshape(n, rows, cols, 3 * chan_in)
            z_ref[frames - n :] += part
    row = jnp.where(core == 0, rows - 1, 0)
    tap_row = jnp.where(core == 0, 0, 2)
    for a in range(3):
        n = frames - 2 + a
        window = edge_ref[2 - a : frames].reshape(n * cols, chan_out)
        part = by_taps(window, w_ref, a * 3 + tap_row, chan_in)
        for t in range(n):
            z_ref[t, row] += part[t * cols : (t + 1) * cols]
    means, inverses = frame_stats(place, stats_ref, frames, per_frame)
    affine = stats_ref[stats_ref.shape[0] - 1]
    gain, bias = affine[:1], affine[1:2]
    col = lax.broadcasted_iota(jnp.int32, (cells, chan_in), 0) % cols
    by_gain = jnp.zeros((1, chan_in), F32)
    by_bias = jnp.zeros((1, chan_in), F32)
    for t in range(frames):
        z = z_ref[t].reshape(cells, 3 * chan_in)
        left = jnp.where(col == cols - 1, 0.0, pltpu.roll(z[:, :chan_in], cells - 1, 0))
        right = jnp.where(col == 0, 0.0, pltpu.roll(z[:, 2 * chan_in :], 1, 0))
        grad_hidden = left + z[:, chan_in : 2 * chan_in] + right
        normed = (x_ref[t].astype(F32) - means[2 + t]) * inverses[2 + t]
        act = normed * gain + bias
        sigma = lax.logistic(act)
        grad_act = grad_hidden * sigma * (1.0 + act * (1.0 - sigma))
        by_gain = by_gain + jnp.sum(grad_act * normed, axis=0, keepdims=True)
        by_bias = by_bias + jnp.sum(grad_act, axis=0, keepdims=True)
    o_ref[...] = jnp.concatenate([by_gain, by_bias], axis=0)


def kernel_grad_kernel(
    per_frame, late, skip, place, stats_ref, next_ref, edge_ref, edge_next, x_ref, g_ref, *rest
):
    keep_ref, send_ref, ht_ref, gp_ref = rest
    frames, cells, chan_in = x_ref.shape
    rows, cols, chan_out = g_ref.shape[1:]
    core = place[1]
    pad_rows(core, g_ref[...], edge_ref[...], gp_ref.at[:frames])
    pad_rows(core, next_ref[...], edge_next[:, :, :chan_out], gp_ref.at[frames:])
    means, inverses = frame_stats(place, stats_ref, frames, per_frame)
    affine = stats_ref[stats_ref.shape[0] - 1]
    gain, bias = affine[:1], affine[1:2]
    block = 2 * cols
    lane = lax.broadcasted_iota(jnp.int32, (chan_in, block), 1) % cols
    for t in range(frames):
        for half in range(cells // block):
            v = x_ref[t, half * block : (half + 1) * block].astype(F32)
            act = (v - means[2 + t]) * inverses[2 + t] * gain + bias
            hidden = (act * lax.logistic(act)).astype(BF16).astype(F32)
            turned = hidden.T
            at = t * cells + half * block
            earlier = jnp.where(lane == 0, 0.0, pltpu.roll(turned, 1, 1))
            later = jnp.where(lane == cols - 1, 0.0, pltpu.roll(turned, block - 1, 1))
            for d, piece in enumerate((earlier, turned, later)):
                piece = piece.astype(BF16)
                for k in range(chan_in // 16):
                    to = late(d * (chan_in // 16) + k) * 16
                    ht_ref[to : to + 16, at : at + block] = piece[k * 16 : (k + 1) * 16]
    mine = chan_out // 2
    n = 3 * chan_in
    for a in range(3):
        for b in range(3):
            tap = a * 3 + b
            window = gp_ref[2 - a : 2 - a + frames, 2 - b : 2 - b + rows].reshape(frames * cells, chan_out)
            part = jnp.dot(ht_ref[...], window, preferred_element_type=F32)
            low, high = part[:, :mine], part[:, mine:]
            keep = jnp.where(core == 0, low, high)
            send = jnp.where(core == 0, high, low).astype(BF16)
            for begin, end, at in ((0, skip, tap * skip), (skip, n, 9 * skip + tap * (n - skip))):
                if end > begin:
                    keep_ref[at : at + end - begin] = keep[begin:end]
                    send_ref[at : at + end - begin] = send[begin:end]


def hidden_kernel(
    per_frame, place, stats_ref, x_ref, prev_ref, edge_ref, prev_edge, h_ref
):
    frames, rows, cols, chan_in = x_ref.shape
    mine, core = place[0], place[1]
    means, inverses = frame_stats(place, stats_ref, frames, per_frame)
    affine = stats_ref[stats_ref.shape[0] - 1]
    gain, bias = affine[:1], affine[1:2]

    def put(f, r0, rows_now, value, keep):
        act = (value.astype(F32) - means[f]) * inverses[f] * gain + bias
        hidden = act * lax.logistic(act)
        if keep is not None:
            hidden = jnp.where(keep, hidden, 0.0)
        n = rows_now * cols
        col = lax.broadcasted_iota(jnp.int32, (n, chan_in), 0) % cols
        earlier = jnp.where(col == 0, 0.0, pltpu.roll(hidden, 1, 0))
        later = jnp.where(col == cols - 1, 0.0, pltpu.roll(hidden, n - 1, 0))
        for d, piece in enumerate((earlier, hidden, later)):
            h_ref[f, r0 : r0 + rows_now, :, d * chan_in : (d + 1) * chan_in] = piece.astype(BF16).reshape(
                rows_now, cols, chan_in
            )

    for f in range(frames + 2):
        inside = (mine > 0) if f < 2 else None
        value = prev_ref[f] if f < 2 else x_ref[f - 2]
        put(f, 1, rows, value.reshape(rows * cols, chan_in), inside)
        for r0, here in ((0, core == 1), (rows + 1, core == 0)):
            put(f, r0, 1, prev_edge[f, :, prev_edge.shape[2] - chan_in :] if f < 2 else edge_ref[f - 2], here if inside is None else jnp.logical_and(here, inside))


def output_kernel(h_ref, w_ref, o_ref, acc_ref):
    frames, rows, cols, size = h_ref.shape
    frames, rows = frames - 2, rows - 2
    cells = frames * rows * cols
    for a in range(3):
        for b in range(3):
            tap = a * 3 + b
            window = h_ref[a : a + frames, b : b + rows].reshape(cells, size)
            part = jnp.dot(window, w_ref[tap * size : (tap + 1) * size], preferred_element_type=F32)
            if tap == 0:
                acc_ref[...] = part
            elif tap < 8:
                acc_ref[...] += part
            else:
                o_ref[...] = (acc_ref[...] + part).astype(BF16)


def split_kernel(cut, rest, place, keep_ref, recv_ref, stay1, send1, stay2, *send2):
    tm = len(send2) + 1

    def total(at):
        rows = pl.ds(pl.multiple_of(at, 16), size)
        return keep_ref[rows] + recv_ref[rows].astype(F32)

    size = rest
    stay2[...] = total(place[0] * rest)
    for k, send in zip(OTHERS, send2):
        send[...] = total(jnp.bitwise_xor(place[0], k) * rest).astype(BF16)
    size = cut
    for t in range(tm):
        at = tm * rest + 2 * t * cut
        stay1[t * cut : (t + 1) * cut] = total(at + place[2] * cut)
        send1[t * cut : (t + 1) * cut] = total(at + (1 - place[2]) * cut).astype(BF16)


def put_rider(rider, dst, at):
    parts = []
    for _ in range(3):
        part = rider.astype(BF16)
        rider = rider - part.astype(F32)
        parts.append(part.astype(F32))
    parts.append(jnp.zeros((16 - 3 * rider.shape[0], rider.shape[1]), F32))
    dst[at : at + 16] = jnp.concatenate(parts, axis=0).astype(BF16)


def get_rider(src, at, n):
    rows = src[at : at + 16].astype(F32)
    return (rows[:n] + rows[n : 2 * n]) + rows[2 * n : 3 * n]


def middle_kernel(place, stay1_ref, recv1_ref, stay2_ref, b_ref, c_ref, a_ref, rider_ref, got_ref, *outs):
    stay1, sends, stay2, send2, rider_out = outs[0], outs[1:4], outs[4], outs[5], outs[6]
    rider = rider_ref[...] + got_ref[...]
    rider_out[...] = rider
    n = stay1.shape[0]

    def total(other):
        rows = pl.ds(pl.multiple_of(jnp.bitwise_xor(place[0], other) * n, 16), n)
        return stay1_ref[rows] + recv1_ref[rows].astype(F32)

    stay1[...] = total(0)
    for k, send in zip(OTHERS, sends):
        send[:n] = total(k).astype(BF16)
        put_rider(rider, send, n)
    m = stay2.shape[0]

    def summed(bit):
        rows = pl.ds(pl.multiple_of(bit * m, 16), m)
        first = stay2_ref[rows] + a_ref[rows].astype(F32)
        return first + (b_ref[rows].astype(F32) + c_ref[rows].astype(F32))

    stay2[...] = summed(place[2])
    send2[...] = summed(1 - place[2]).astype(BF16)


def last_kernel(stay1_ref, b_ref, c_ref, a_ref, stay2_ref, recv2_ref, rider_ref, o_ref, gain_ref, bias_ref):
    for k in range(stay2_ref.shape[0] // 16):
        two, one = slice(16 * k, 16 * k + 16), slice(32 * k, 32 * k + 32)
        near = stay1_ref[one] + a_ref[one].astype(F32)
        o_ref[48 * k : 48 * k + 32] = near + (b_ref[one].astype(F32) + c_ref[one].astype(F32))
        o_ref[48 * k + 32 : 48 * k + 48] = stay2_ref[two] + recv2_ref[two].astype(F32)
    n = stay1_ref.shape[0]
    near, b, c = (get_rider(ref, n, 2) for ref in (a_ref, b_ref, c_ref))
    rider = (rider_ref[...] + near) + (b + c)
    gain_ref[...] = rider[:1]
    bias_ref[...] = rider[1:]


def bits_of(axis):
    return [1 << k for k in range((lax.axis_size(axis) - 1).bit_length())]


def swap(value, axis, step):
    return lax.ppermute(value, axis, [(i, i ^ step) for i in range(lax.axis_size(axis))])


def together(*values):
    return lax.optimization_barrier(values)


def all_sum(value, axes):
    for axis in axes:
        for step in bits_of(axis):
            value = value + swap(value, axis, step)
    return value


def parted(value, axis, step):
    value = value.reshape((value.shape[0] // 2, 2) + value.shape[1:])
    bit = jnp.minimum(jnp.bitwise_and(lax.axis_index(axis), step), 1)
    keep = lax.dynamic_index_in_dim(value, bit, 1, keepdims=False)
    send = lax.dynamic_index_in_dim(value, 1 - bit, 1, keepdims=False)
    return keep, send.astype(BF16)


def body(clips, gain, bias, weight, cotangent):
    x, g = clips[0], cotangent[0]
    frames, rows, cols, chan_in = x.shape
    chan_out = g.shape[-1]
    per_group = chan_in // GROUPS
    tm, dp, width = (lax.axis_size(name) for name in ("tm", "dp", "width"))
    per_frame = float(rows * width * cols * per_group)
    z, core = lax.axis_index("tm"), lax.axis_index("width")
    place = jnp.stack([z, core, lax.axis_index("dp")]).astype(jnp.int32)
    cells = rows * cols
    shape = jax.ShapeDtypeStruct
    half = chan_out // 2

    odd_pairs = [(i, i ^ 1) for i in range(tm)]
    even_pairs = [(i, i + 1 if i % 2 else i - 1) for i in range(1, tm - 1)]
    affine = jnp.pad(jnp.stack([gain, bias]), ((0, 2 * frames - 2), (0, 0)))[None]
    x, g, place = together(x, g, place)
    sums, to_odd, to_even, g_rows, x_rows, x_near, g_near = call(
        functools.partial(prepare_kernel, per_group),
        (
            shape((2 * frames, chan_in), F32),
            shape((2 * cells + 4 * frames, chan_out), BF16),
            shape((2, rows, cols, chan_out), BF16),
            shape((frames, cols, chan_out), BF16),
            shape((frames, cols, chan_in), BF16),
            shape(x.shape, BF16),
            shape(g.shape, BF16),
        ),
        [place, far(x), far(g)],
        [pltpu.SemaphoreType.DMA((2 * frames,))],
        scalars=1,
        far=2,
    )
    from_odd = lax.ppermute(to_odd, "tm", odd_pairs)
    from_even = lax.ppermute(to_even, "tm", even_pairs)
    g_edge = swap(g_rows, "width", 1)
    x_edge = swap(x_rows, "width", 1)
    x, g = x_near, g_near
    flat = x.reshape(frames, cells, chan_in)
    sums, g = together(sums, g)
    own_grad = call(
        own_grad_kernel,
        shape((frames, rows, cols, 3 * chan_in), F32),
        [g, weight],
        [pltpu.VMEM((frames, rows + 2, cols, chan_out), BF16)],
    )
    sums, from_odd, from_even, g_edge, x_edge, own_grad = together(sums, from_odd, from_even, g_edge, x_edge, own_grad)

    g_next, x_prev, next_edge = call(
        arrived_kernel,
        (
            shape((2, rows, cols, chan_out), BF16),
            shape((2, rows, cols, chan_in), BF16),
            shape((2, cols, chan_out + chan_in), BF16),
        ),
        [place, from_odd, from_even],
        scalars=1,
    )
    next_edge = swap(next_edge, "width", 1)
    near = from_odd[2 * cells :].astype(F32)
    near = (near[: 2 * frames, :chan_in] + near[2 * frames :, :chan_in]) + near[: 2 * frames, chan_in:]
    stats = jnp.stack([sums, near])
    for step in bits_of("tm")[1:]:
        stats = jnp.concatenate([stats, swap(stats, "tm", step)], axis=0)
    stats, next_edge, g_next, x_prev = together(stats, next_edge, g_next, x_prev)
    stats = stats + swap(stats, "width", 1)
    stats = jnp.concatenate([stats, affine], axis=0)

    share = 27 * chan_in // (tm * dp)
    pieces = share % 48 == 0 and tm == 4 and dp == 2
    count = 3 * chan_in // 48
    if pieces:
        skip = chan_in
        late = lambda k: k // 3 if k % 3 == 2 else count + k // 3 * 2 + k % 3
    else:
        skip = 0
        late = lambda k: k
    keep, send = call(
        functools.partial(kernel_grad_kernel, per_frame, late, skip),
        (shape((27 * chan_in, half), F32), shape((27 * chan_in, half), BF16)),
        [place, stats, g_next, g_edge, next_edge, flat, g],
        [
            pltpu.VMEM((3 * chan_in, frames * cells), BF16),
            pltpu.VMEM((frames + 2, rows + 2, cols, chan_out), BF16),
        ],
        scalars=1,
    )
    send, hold = together(send, stats)
    recv = swap(send, "width", 1)
    local = call(
        functools.partial(gain_kernel, per_frame),
        shape((2, chan_in), F32),
        [place, hold, flat, own_grad, g_next, g_edge, next_edge, weight],
        [
            pltpu.VMEM((2, rows + 2, cols, chan_out), BF16),
            pltpu.VMEM((frames, rows, cols, 3 * chan_in), F32),
        ],
        scalars=1,
    )
    recv, local = together(recv, local)

    def activations(hold):
        return call(
            functools.partial(hidden_kernel, per_frame),
            shape((frames + 2, rows + 2, cols, 3 * chan_in), BF16),
            [place, hold, x, x_prev, x_edge, next_edge],
            scalars=1,
        )

    def outputs(hidden):
        return call(
            output_kernel,
            shape((frames * cells, chan_out), BF16),
            [hidden, weight],
            [pltpu.VMEM((frames * cells, chan_out), F32)],
        )

    if not pieces:
        output = outputs(activations(stats))
        one = keep + recv.astype(F32)
        one = jnp.moveaxis(one.reshape(tm, dp, share, half), 1, 0)
        for step in bits_of("dp"):
            one, send = parted(one, "dp", step)
            one = one + swap(send, "dp", step).astype(F32)
        one = one[0]
        for step in bits_of("tm"):
            one, send = parted(one, "tm", step)
            one = one + swap(send, "tm", step).astype(F32)
        rider = all_sum(local, ("width", "dp", "tm"))
        grad_weight = one[0]
    else:
        rest = share // 3
        cut = share - rest

        def piece(n, kind):
            return shape((n, half), kind)

        both = dp * rest
        stay1, send1, stay2, *send2 = call(
            functools.partial(split_kernel, cut, both),
            [piece(tm * cut, F32), piece(tm * cut, BF16), piece(both, F32)] + [piece(both, BF16)] * (tm - 1),
            [place, keep, recv],
            scalars=1,
        )
        rider = local + swap(local, "width", 1)
        send1, hold, rider, *send2 = together(send1, hold, rider, *send2)
        recv2 = [swap(send2[0], "tm", OTHERS[0])]
        recv1 = swap(send1, "dp", 1)
        recv2 += [swap(v, "tm", k) for k, v in zip(OTHERS[1:], send2[1:])]
        got = swap(rider, "dp", 1)
        recv1, got, hidden, *recv2 = together(recv1, got, activations(hold), *recv2)
        stay1, *send1, stay2, send2, rider = call(
            middle_kernel,
            [piece(cut, F32)]
            + [piece(cut + 16, BF16)] * (tm - 1)
            + [piece(rest, F32), piece(rest, BF16), shape(rider.shape, F32)],
            [place, stay1, recv1, stay2, *recv2, rider, got],
            scalars=1,
        )
        send2, hidden, *send1 = together(send2, hidden, *send1)
        recv1 = [swap(v, "tm", k) for k, v in zip(OTHERS, send1)]
        recv2 = swap(send2, "dp", 1)
        output = outputs(hidden)
        recv2, output, *recv1 = together(recv2, output, *recv1)
        row = shape((1, chan_in), F32)
        grad_weight, *rider = call(
            last_kernel, [piece(share, F32), row, row], [stay1, *recv1, stay2, recv2, rider]
        )
        rider = [v.reshape(chan_in) for v in rider]
    return (output.reshape(1, frames, rows, cols, chan_out), grad_weight, rider[0], rider[1])


def solution(mesh):
    return jax.shard_map(
        body,
        mesh=mesh,
        in_specs=(
            P(("groups", "dp"), "tm", "width", None, None),
            P(),
            P(),
            P(),
            P(("groups", "dp"), "tm", "width", None, None),
        ),
        out_specs=(
            P(("groups", "dp"), "tm", "width", None, None),
            P(("groups", "tm", "dp"), "width"),
            P("groups"),
            P("groups"),
        ),
        check_vma=False,
    )
```

```python
import functools

import jax
import jax.numpy as jnp
from jax import lax
from jax.experimental import pallas as pl
from jax.experimental.pallas import tpu as pltpu
from jax.sharding import PartitionSpec as P

GROUPS = 32
OTHERS = (2, 3, 1)
F32, BF16 = jnp.float32, jnp.bfloat16
VMEM = pl.BlockSpec(memory_space=pltpu.VMEM)
SMEM = pl.BlockSpec(memory_space=pltpu.SMEM)
HBM = pl.BlockSpec(memory_space=pltpu.HBM)


def call(kernel, out_shape, inputs, scratch=(), flops=0, scalars=0, far=0):
    outs = jax.tree.leaves(out_shape)
    moved = sum(v.size * v.dtype.itemsize for v in list(inputs) + list(outs))
    return pl.pallas_call(
        kernel,
        out_shape=out_shape,
        in_specs=[SMEM] * scalars + [VMEM] * (len(inputs) - scalars - far) + [HBM] * far,
        out_specs=jax.tree.map(lambda _: VMEM, out_shape),
        scratch_shapes=list(scratch),
        cost_estimate=pl.CostEstimate(flops=0, bytes_accessed=moved, transcendentals=0),
        compiler_params=pltpu.CompilerParams(vmem_limit_bytes=16 << 20),
    )(*inputs)


def far(value):
    return pltpu.with_memory_space_constraint(value, pltpu.HBM)


def group_sum(rows, per_group):
    lane = lax.broadcasted_iota(jnp.int32, rows.shape, 1)
    lanes = rows.shape[1]
    step = 1
    while step < per_group:
        up = pltpu.roll(rows, lanes - step, 1)
        down = pltpu.roll(rows, step, 1)
        rows = rows + jnp.where((lane // step) % 2 == 0, up, down)
        step *= 2
    return rows


def prepare_kernel(per_group, place, x_hbm, g_hbm, sums_ref, odd_ref, even_ref, row_ref, x_row_ref, x_ref, g_ref, sems):
    frames, rows, cols, chan_in = x_ref.shape
    row = jnp.where(place[1] == 0, rows - 1, 0)
    copies = [pltpu.make_async_copy(x_hbm.at[t], x_ref.at[t], sems.at[t]) for t in range(frames)]
    copies += [pltpu.make_async_copy(g_hbm.at[t], g_ref.at[t], sems.at[frames + t]) for t in range(frames)]
    for copy in copies:
        copy.start()
    firsts, squares = [], []
    for t in range(frames):
        copies[t].wait()
        v = x_ref[t].reshape(rows * cols, chan_in).astype(F32)
        firsts.append(jnp.sum(v, axis=0, keepdims=True))
        squares.append(jnp.sum(v * v, axis=0, keepdims=True))
        x_row_ref[t] = x_ref[t, row]
    total = group_sum(jnp.concatenate(firsts + squares, axis=0), per_group)
    sums_ref[...] = total
    parts = []
    for _ in range(3):
        parts.append(total.astype(BF16).astype(F32))
        total = total - parts[-1]
    n = rows * cols
    odd_ref[2 * n :, :chan_in] = jnp.concatenate(parts[:2], axis=0).astype(BF16)
    odd_ref[2 * n :, chan_in:] = jnp.concatenate([parts[2], jnp.zeros_like(total)], axis=0).astype(BF16)
    for t in range(frames):
        copies[frames + t].wait()
        row_ref[t] = g_ref[t, row]
    even = jnp.bitwise_and(place[0], 1) == 0
    for t in range(2):
        clip, low = x_ref[frames - 2 + t], g_ref[t, :, :, :chan_in]
        here = slice(t * n, (t + 1) * n)
        odd_ref[here, :chan_in] = jnp.where(even, clip, low).reshape(n, chan_in)
        even_ref[t, :, :, :chan_in] = jnp.where(even, low, clip)
        odd_ref[here, chan_in:] = g_ref[t, :, :, chan_in:].reshape(n, chan_in)
        even_ref[t, :, :, chan_in:] = g_ref[t, :, :, chan_in:]


def arrived_kernel(place, odd_ref, even_ref, next_ref, prev_ref, edge_ref):
    chan_in, chan_out = prev_ref.shape[3], next_ref.shape[3]
    even = jnp.bitwise_and(place[0], 1) == 0
    row = jnp.where(place[1] == 0, next_ref.shape[1] - 1, 0)
    n = next_ref.shape[1] * next_ref.shape[2]
    for t in range(2):
        odd = odd_ref[t * n : (t + 1) * n].reshape(next_ref.shape[1:])
        next_ref[t] = jnp.where(even, odd, even_ref[t])
        prev_ref[t] = jnp.where(even, even_ref[t, :, :, :chan_in], odd[:, :, :chan_in])
        edge_ref[t, :, :chan_out] = next_ref[t, row]
        edge_ref[t, :, chan_out:] = prev_ref[t, row]


def frame_stats(place, stats_ref, frames, per_frame):
    devices = stats_ref.shape[0] - 1
    mine = place[0]
    own = stats_ref[0]
    before = jnp.zeros_like(own)
    behind = jnp.zeros_like(own)
    for x in range(1, devices):
        other = jnp.bitwise_xor(mine, x)
        rows = stats_ref[x]
        before = before + jnp.where(other < mine - 1, rows, 0.0)
        behind = behind + jnp.where(other == mine - 1, rows, 0.0)

    def total(rows, at):
        return jnp.sum(rows[at : at + frames], axis=0, keepdims=True)

    first, square = total(before, 0), total(before, frames)
    means, inverses = [], []
    for k in range(2 * frames):
        rows, t = (behind, k) if k < frames else (own, k - frames)
        first = first + rows[t : t + 1]
        square = square + rows[frames + t : frames + t + 1]
        if k < frames - 2:
            continue
        shown = jnp.maximum(mine * frames + k - frames + 1, 1).astype(F32) * per_frame
        mean = first / shown
        variance = square / shown - mean * mean
        means.append(mean)
        inverses.append(lax.rsqrt(variance + 1e-05))
    return means, inverses


def pad_rows(core, own, edge, dst):
    rows = own.shape[1]
    zero = jnp.zeros_like(edge)
    dst[:, 0] = jnp.where(core == 0, zero, edge)
    dst[:, rows + 1] = jnp.where(core == 0, edge, zero)
    dst[:, 1 : rows + 1] = own


def by_taps(window, w_ref, tap, chan_in):
    size = 3 * chan_in
    start = tap * size if isinstance(tap, int) else pl.multiple_of(tap * size, size)
    return lax.dot_general(
        window, w_ref[pl.ds(start, size)], (((1,), (1,)), ((), ())), preferred_element_type=F32
    )


def own_grad_kernel(g_ref, w_ref, z_ref, gp_ref):
    frames, rows, cols, chan_out = g_ref.shape
    chan_in = z_ref.shape[3] // 3
    zero = jnp.zeros((frames, cols, chan_out), BF16)
    gp_ref[:, 0] = zero
    gp_ref[:, rows + 1] = zero
    gp_ref[:, 1 : rows + 1] = g_ref[...]
    for a in (2, 1, 0):
        n = frames - 2 + a
        for b in range(3):
            window = gp_ref[2 - a :, 2 - b : 2 - b + rows].reshape(n * rows * cols, chan_out)
            part = by_taps(window, w_ref, a * 3 + b, chan_in).reshape(n, rows, cols, 3 * chan_in)
            if a == 2 and b == 0:
                z_ref[...] = part
            else:
                z_ref[:n] += part


def gain_kernel(
    per_frame, place, stats_ref, x_ref, own_ref, next_ref, edge_ref, edge_next, w_ref, o_ref, gp_ref, z_ref
):
    frames, rows, cols, chan_out = own_ref.shape[:3] + (next_ref.shape[3],)
    chan_in = x_ref.shape[2]
    cells = rows * cols
    core = place[1]
    pad_rows(core, next_ref[...], edge_next[:, :, :chan_out], gp_ref)
    z_ref[...] = own_ref[...]
    for a in range(2):
        n = 2 - a
        for b in range(3):
            window = gp_ref[:n, 2 - b : 2 - b + rows].reshape(n * cells, chan_out)
            part = by_taps(window, w_ref, a * 3 + b, chan_in).reshape(n, rows, cols, 3 * chan_in)
            z_ref[frames - n :] += part
    row = jnp.where(core == 0, rows - 1, 0)
    tap_row = jnp.where(core == 0, 0, 2)
    for a in range(3):
        n = frames - 2 + a
        window = edge_ref[2 - a : frames].reshape(n * cols, chan_out)
        part = by_taps(window, w_ref, a * 3 + tap_row, chan_in)
        for t in range(n):
            z_ref[t, row] += part[t * cols : (t + 1) * cols]
    means, inverses = frame_stats(place, stats_ref, frames, per_frame)
    affine = stats_ref[stats_ref.shape[0] - 1]
    gain, bias = affine[:1], affine[1:2]
    col = lax.broadcasted_iota(jnp.int32, (cells, chan_in), 0) % cols
    by_gain = jnp.zeros((1, chan_in), F32)
    by_bias = jnp.zeros((1, chan_in), F32)
    for t in range(frames):
        z = z_ref[t].reshape(cells, 3 * chan_in)
        left = jnp.where(col == cols - 1, 0.0, pltpu.roll(z[:, :chan_in], cells - 1, 0))
        right = jnp.where(col == 0, 0.0, pltpu.roll(z[:, 2 * chan_in :], 1, 0))
        grad_hidden = left + z[:, chan_in : 2 * chan_in] + right
        normed = (x_ref[t].astype(F32) - means[2 + t]) * inverses[2 + t]
        act = normed * gain + bias
        sigma = lax.logistic(act)
        grad_act = grad_hidden * sigma * (1.0 + act * (1.0 - sigma))
        by_gain = by_gain + jnp.sum(grad_act * normed, axis=0, keepdims=True)
        by_bias = by_bias + jnp.sum(grad_act, axis=0, keepdims=True)
    o_ref[...] = jnp.concatenate([by_gain, by_bias], axis=0)


def kernel_grad_kernel(
    per_frame, late, skip, place, stats_ref, next_ref, edge_ref, edge_next, x_ref, g_ref, *rest
):
    keep_ref, send_ref, ht_ref, gp_ref = rest
    frames, cells, chan_in = x_ref.shape
    rows, cols, chan_out = g_ref.shape[1:]
    core = place[1]
    pad_rows(core, g_ref[...], edge_ref[...], gp_ref.at[:frames])
    pad_rows(core, next_ref[...], edge_next[:, :, :chan_out], gp_ref.at[frames:])
    means, inverses = frame_stats(place, stats_ref, frames, per_frame)
    affine = stats_ref[stats_ref.shape[0] - 1]
    gain, bias = affine[:1], affine[1:2]
    block = 2 * cols
    lane = lax.broadcasted_iota(jnp.int32, (chan_in, block), 1) % cols
    for t in range(frames):
        for half in range(cells // block):
            v = x_ref[t, half * block : (half + 1) * block].astype(F32)
            act = (v - means[2 + t]) * inverses[2 + t] * gain + bias
            hidden = (act * lax.logistic(act)).astype(BF16).astype(F32)
            turned = hidden.T
            at = t * cells + half * block
            earlier = jnp.where(lane == 0, 0.0, pltpu.roll(turned, 1, 1))
            later = jnp.where(lane == cols - 1, 0.0, pltpu.roll(turned, block - 1, 1))
            for d, piece in enumerate((earlier, turned, later)):
                piece = piece.astype(BF16)
                for k in range(chan_in // 16):
                    to = late(d * (chan_in // 16) + k) * 16
                    ht_ref[to : to + 16, at : at + block] = piece[k * 16 : (k + 1) * 16]
    mine = chan_out // 2
    n = 3 * chan_in
    for a in range(3):
        for b in range(3):
            tap = a * 3 + b
            window = gp_ref[2 - a : 2 - a + frames, 2 - b : 2 - b + rows].reshape(frames * cells, chan_out)
            part = jnp.dot(ht_ref[...], window, preferred_element_type=F32)
            low, high = part[:, :mine], part[:, mine:]
            keep = jnp.where(core == 0, low, high)
            send = jnp.where(core == 0, high, low).astype(BF16)
            for begin, end, at in ((0, skip, tap * skip), (skip, n, 9 * skip + tap * (n - skip))):
                if end > begin:
                    keep_ref[at : at + end - begin] = keep[begin:end]
                    send_ref[at : at + end - begin] = send[begin:end]


def hidden_kernel(
    per_frame, place, stats_ref, x_ref, prev_ref, edge_ref, prev_edge, h_ref
):
    frames, rows, cols, chan_in = x_ref.shape
    mine, core = place[0], place[1]
    means, inverses = frame_stats(place, stats_ref, frames, per_frame)
    affine = stats_ref[stats_ref.shape[0] - 1]
    gain, bias = affine[:1], affine[1:2]

    def put(f, r0, rows_now, value, keep):
        act = (value.astype(F32) - means[f]) * inverses[f] * gain + bias
        hidden = act * lax.logistic(act)
        if keep is not None:
            hidden = jnp.where(keep, hidden, 0.0)
        n = rows_now * cols
        col = lax.broadcasted_iota(jnp.int32, (n, chan_in), 0) % cols
        earlier = jnp.where(col == 0, 0.0, pltpu.roll(hidden, 1, 0))
        later = jnp.where(col == cols - 1, 0.0, pltpu.roll(hidden, n - 1, 0))
        for d, piece in enumerate((earlier, hidden, later)):
            h_ref[f, r0 : r0 + rows_now, :, d * chan_in : (d + 1) * chan_in] = piece.astype(BF16).reshape(
                rows_now, cols, chan_in
            )

    for f in range(frames + 2):
        inside = (mine > 0) if f < 2 else None
        value = prev_ref[f] if f < 2 else x_ref[f - 2]
        put(f, 1, rows, value.reshape(rows * cols, chan_in), inside)
        for r0, here in ((0, core == 1), (rows + 1, core == 0)):
            put(f, r0, 1, prev_edge[f, :, prev_edge.shape[2] - chan_in :] if f < 2 else edge_ref[f - 2], here if inside is None else jnp.logical_and(here, inside))


def output_kernel(h_ref, w_ref, o_ref, acc_ref):
    frames, rows, cols, size = h_ref.shape
    frames, rows = frames - 2, rows - 2
    cells = frames * rows * cols
    for a in range(3):
        for b in range(3):
            tap = a * 3 + b
            window = h_ref[a : a + frames, b : b + rows].reshape(cells, size)
            part = jnp.dot(window, w_ref[tap * size : (tap + 1) * size], preferred_element_type=F32)
            if tap == 0:
                acc_ref[...] = part
            elif tap < 8:
                acc_ref[...] += part
            else:
                o_ref[...] = (acc_ref[...] + part).astype(BF16)


def split_kernel(cut, rest, place, keep_ref, recv_ref, stay1, send1, stay2, *send2):
    tm = len(send2) + 1

    def total(at):
        rows = pl.ds(pl.multiple_of(at, 16), size)
        return keep_ref[rows] + recv_ref[rows].astype(F32)

    size = rest
    stay2[...] = total(place[0] * rest)
    for k, send in zip(OTHERS, send2):
        send[...] = total(jnp.bitwise_xor(place[0], k) * rest).astype(BF16)
    size = cut
    for t in range(tm):
        at = tm * rest + 2 * t * cut
        stay1[t * cut : (t + 1) * cut] = total(at + place[2] * cut)
        send1[t * cut : (t + 1) * cut] = total(at + (1 - place[2]) * cut).astype(BF16)


def put_rider(rider, dst, at):
    parts = []
    for _ in range(3):
        part = rider.astype(BF16)
        rider = rider - part.astype(F32)
        parts.append(part.astype(F32))
    parts.append(jnp.zeros((16 - 3 * rider.shape[0], rider.shape[1]), F32))
    dst[at : at + 16] = jnp.concatenate(parts, axis=0).astype(BF16)


def get_rider(src, at, n):
    rows = src[at : at + 16].astype(F32)
    return (rows[:n] + rows[n : 2 * n]) + rows[2 * n : 3 * n]


def middle_kernel(place, stay1_ref, recv1_ref, stay2_ref, b_ref, c_ref, a_ref, rider_ref, got_ref, *outs):
    stay1, sends, stay2, send2, rider_out = outs[0], outs[1:4], outs[4], outs[5], outs[6]
    rider = rider_ref[...] + got_ref[...]
    rider_out[...] = rider
    n = stay1.shape[0]

    def total(other):
        rows = pl.ds(pl.multiple_of(jnp.bitwise_xor(place[0], other) * n, 16), n)
        return stay1_ref[rows] + recv1_ref[rows].astype(F32)

    stay1[...] = total(0)
    for k, send in zip(OTHERS, sends):
        send[:n] = total(k).astype(BF16)
        put_rider(rider, send, n)
    m = stay2.shape[0]

    def summed(bit):
        rows = pl.ds(pl.multiple_of(bit * m, 16), m)
        first = stay2_ref[rows] + a_ref[rows].astype(F32)
        return first + (b_ref[rows].astype(F32) + c_ref[rows].astype(F32))

    stay2[...] = summed(place[2])
    send2[...] = summed(1 - place[2]).astype(BF16)


def last_kernel(stay1_ref, b_ref, c_ref, a_ref, stay2_ref, recv2_ref, rider_ref, o_ref, gain_ref, bias_ref):
    for k in range(stay2_ref.shape[0] // 16):
        two, one = slice(16 * k, 16 * k + 16), slice(32 * k, 32 * k + 32)
        near = stay1_ref[one] + a_ref[one].astype(F32)
        o_ref[48 * k : 48 * k + 32] = near + (b_ref[one].astype(F32) + c_ref[one].astype(F32))
        o_ref[48 * k + 32 : 48 * k + 48] = stay2_ref[two] + recv2_ref[two].astype(F32)
    n = stay1_ref.shape[0]
    near, b, c = (get_rider(ref, n, 2) for ref in (a_ref, b_ref, c_ref))
    rider = (rider_ref[...] + near) + (b + c)
    gain_ref[...] = rider[:1]
    bias_ref[...] = rider[1:]


def bits_of(axis):
    return [1 << k for k in range((lax.axis_size(axis) - 1).bit_length())]


def swap(value, axis, step):
    return lax.ppermute(value, axis, [(i, i ^ step) for i in range(lax.axis_size(axis))])


def together(*values):
    return lax.optimization_barrier(values)


def all_sum(value, axes):
    for axis in axes:
        for step in bits_of(axis):
            value = value + swap(value, axis, step)
    return value


def parted(value, axis, step):
    value = value.reshape((value.shape[0] // 2, 2) + value.shape[1:])
    bit = jnp.minimum(jnp.bitwise_and(lax.axis_index(axis), step), 1)
    keep = lax.dynamic_index_in_dim(value, bit, 1, keepdims=False)
    send = lax.dynamic_index_in_dim(value, 1 - bit, 1, keepdims=False)
    return keep, send.astype(BF16)


def body(clips, gain, bias, weight, cotangent):
    x, g = clips[0], cotangent[0]
    frames, rows, cols, chan_in = x.shape
    chan_out = g.shape[-1]
    per_group = chan_in // GROUPS
    tm, dp, width = (lax.axis_size(name) for name in ("tm", "dp", "width"))
    per_frame = float(rows * width * cols * per_group)
    z, core = lax.axis_index("tm"), lax.axis_index("width")
    place = jnp.stack([z, core, lax.axis_index("dp")]).astype(jnp.int32)
    cells = rows * cols
    shape = jax.ShapeDtypeStruct
    half = chan_out // 2

    odd_pairs = [(i, i ^ 1) for i in range(tm)]
    even_pairs = [(i, i + 1 if i % 2 else i - 1) for i in range(1, tm - 1)]
    affine = jnp.pad(jnp.stack([gain, bias]), ((0, 2 * frames - 2), (0, 0)))[None]
    x, g, place = together(x, g, place)
    sums, to_odd, to_even, g_rows, x_rows, x_near, g_near = call(
        functools.partial(prepare_kernel, per_group),
        (
            shape((2 * frames, chan_in), F32),
            shape((2 * cells + 4 * frames, chan_out), BF16),
            shape((2, rows, cols, chan_out), BF16),
            shape((frames, cols, chan_out), BF16),
            shape((frames, cols, chan_in), BF16),
            shape(x.shape, BF16),
            shape(g.shape, BF16),
        ),
        [place, far(x), far(g)],
        [pltpu.SemaphoreType.DMA((2 * frames,))],
        scalars=1,
        far=2,
    )
    from_odd = lax.ppermute(to_odd, "tm", odd_pairs)
    from_even = lax.ppermute(to_even, "tm", even_pairs)
    g_edge = swap(g_rows, "width", 1)
    x_edge = swap(x_rows, "width", 1)
    x, g = x_near, g_near
    flat = x.reshape(frames, cells, chan_in)
    sums, g = together(sums, g)
    own_grad = call(
        own_grad_kernel,
        shape((frames, rows, cols, 3 * chan_in), F32),
        [g, weight],
        [pltpu.VMEM((frames, rows + 2, cols, chan_out), BF16)],
    )
    sums, from_odd, g_edge, x_edge, own_grad = together(sums, from_odd, g_edge, x_edge, own_grad)

    g_next, x_prev, next_edge = call(
        arrived_kernel,
        (
            shape((2, rows, cols, chan_out), BF16),
            shape((2, rows, cols, chan_in), BF16),
            shape((2, cols, chan_out + chan_in), BF16),
        ),
        [place, from_odd, from_even],
        scalars=1,
    )
    next_edge = swap(next_edge, "width", 1)
    near = from_odd[2 * cells :].astype(F32)
    near = (near[: 2 * frames, :chan_in] + near[2 * frames :, :chan_in]) + near[: 2 * frames, chan_in:]
    stats = jnp.stack([sums, near])
    for step in bits_of("tm")[1:]:
        stats = jnp.concatenate([stats, swap(stats, "tm", step)], axis=0)
    stats, next_edge, g_next, x_prev = together(stats, next_edge, g_next, x_prev)
    stats = stats + swap(stats, "width", 1)
    stats = jnp.concatenate([stats, affine], axis=0)

    share = 27 * chan_in // (tm * dp)
    pieces = share % 48 == 0 and tm == 4 and dp == 2
    count = 3 * chan_in // 48
    if pieces:
        skip = chan_in
        late = lambda k: k // 3 if k % 3 == 2 else count + k // 3 * 2 + k % 3
    else:
        skip = 0
        late = lambda k: k
    keep, send = call(
        functools.partial(kernel_grad_kernel, per_frame, late, skip),
        (shape((27 * chan_in, half), F32), shape((27 * chan_in, half), BF16)),
        [place, stats, g_next, g_edge, next_edge, flat, g],
        [
            pltpu.VMEM((3 * chan_in, frames * cells), BF16),
            pltpu.VMEM((frames + 2, rows + 2, cols, chan_out), BF16),
        ],
        scalars=1,
    )
    send, hold = together(send, stats)
    recv = swap(send, "width", 1)
    local = call(
        functools.partial(gain_kernel, per_frame),
        shape((2, chan_in), F32),
        [place, hold, flat, own_grad, g_next, g_edge, next_edge, weight],
        [
            pltpu.VMEM((2, rows + 2, cols, chan_out), BF16),
            pltpu.VMEM((frames, rows, cols, 3 * chan_in), F32),
        ],
        scalars=1,
    )
    recv, local = together(recv, local)

    def activations(hold):
        return call(
            functools.partial(hidden_kernel, per_frame),
            shape((frames + 2, rows + 2, cols, 3 * chan_in), BF16),
            [place, hold, x, x_prev, x_edge, next_edge],
            scalars=1,
        )

    def outputs(hidden):
        return call(
            output_kernel,
            shape((frames * cells, chan_out), BF16),
            [hidden, weight],
            [pltpu.VMEM((frames * cells, chan_out), F32)],
        )

    if not pieces:
        output = outputs(activations(stats))
        one = keep + recv.astype(F32)
        one = jnp.moveaxis(one.reshape(tm, dp, share, half), 1, 0)
        for step in bits_of("dp"):
            one, send = parted(one, "dp", step)
            one = one + swap(send, "dp", step).astype(F32)
        one = one[0]
        for step in bits_of("tm"):
            one, send = parted(one, "tm", step)
            one = one + swap(send, "tm", step).astype(F32)
        rider = all_sum(local, ("width", "dp", "tm"))
        grad_weight = one[0]
    else:
        rest = share // 3
        cut = share - rest

        def piece(n, kind):
            return shape((n, half), kind)

        both = dp * rest
        stay1, send1, stay2, *send2 = call(
            functools.partial(split_kernel, cut, both),
            [piece(tm * cut, F32), piece(tm * cut, BF16), piece(both, F32)] + [piece(both, BF16)] * (tm - 1),
            [place, keep, recv],
            scalars=1,
        )
        rider = local + swap(local, "width", 1)
        send1, hold, rider, *send2 = together(send1, hold, rider, *send2)
        recv2 = [swap(send2[0], "tm", OTHERS[0])]
        recv1 = swap(send1, "dp", 1)
        recv2 += [swap(v, "tm", k) for k, v in zip(OTHERS[1:], send2[1:])]
        got = swap(rider, "dp", 1)
        recv1, got, hidden, *recv2 = together(recv1, got, activations(hold), *recv2)
        stay1, *send1, stay2, send2, rider = call(
            middle_kernel,
            [piece(cut, F32)]
            + [piece(cut + 16, BF16)] * (tm - 1)
            + [piece(rest, F32), piece(rest, BF16), shape(rider.shape, F32)],
            [place, stay1, recv1, stay2, *recv2, rider, got],
            scalars=1,
        )
        send2, hidden, *send1 = together(send2, hidden, *send1)
        recv1 = [swap(v, "tm", k) for k, v in zip(OTHERS, send1)]
        recv2 = swap(send2, "dp", 1)
        output = outputs(hidden)
        recv2, output, *recv1 = together(recv2, output, *recv1)
        row = shape((1, chan_in), F32)
        grad_weight, *rider = call(
            last_kernel, [piece(share, F32), row, row], [stay1, *recv1, stay2, recv2, rider]
        )
        rider = [v.reshape(chan_in) for v in rider]
    return (output.reshape(1, frames, rows, cols, chan_out), grad_weight, rider[0], rider[1])


def solution(mesh):
    return jax.shard_map(
        body,
        mesh=mesh,
        in_specs=(
            P(("groups", "dp"), "tm", "width", None, None),
            P(),
            P(),
            P(),
            P(("groups", "dp"), "tm", "width", None, None),
        ),
        out_specs=(
            P(("groups", "dp"), "tm", "width", None, None),
            P(("groups", "tm", "dp"), "width"),
            P("groups"),
            P("groups"),
        ),
        check_vma=False,
    )
```

```python
import functools

import jax
import jax.numpy as jnp
from jax import lax
from jax.experimental import pallas as pl
from jax.experimental.pallas import tpu as pltpu
from jax.sharding import PartitionSpec as P

GROUPS = 32
OTHERS = (2, 3, 1)
F32, BF16 = jnp.float32, jnp.bfloat16
VMEM = pl.BlockSpec(memory_space=pltpu.VMEM)
SMEM = pl.BlockSpec(memory_space=pltpu.SMEM)
HBM = pl.BlockSpec(memory_space=pltpu.HBM)


def call(kernel, out_shape, inputs, scratch=(), flops=0, scalars=0, far=0):
    outs = jax.tree.leaves(out_shape)
    moved = sum(v.size * v.dtype.itemsize for v in list(inputs) + list(outs))
    return pl.pallas_call(
        kernel,
        out_shape=out_shape,
        in_specs=[SMEM] * scalars + [VMEM] * (len(inputs) - scalars - far) + [HBM] * far,
        out_specs=jax.tree.map(lambda _: VMEM, out_shape),
        scratch_shapes=list(scratch),
        cost_estimate=pl.CostEstimate(flops=0, bytes_accessed=moved, transcendentals=0),
        compiler_params=pltpu.CompilerParams(vmem_limit_bytes=16 << 20),
    )(*inputs)


def far(value):
    return pltpu.with_memory_space_constraint(value, pltpu.HBM)


def group_sum(rows, per_group):
    lane = lax.broadcasted_iota(jnp.int32, rows.shape, 1)
    lanes = rows.shape[1]
    step = 1
    while step < per_group:
        up = pltpu.roll(rows, lanes - step, 1)
        down = pltpu.roll(rows, step, 1)
        rows = rows + jnp.where((lane // step) % 2 == 0, up, down)
        step *= 2
    return rows


def prepare_kernel(per_group, place, x_hbm, g_hbm, sums_ref, odd_ref, even_ref, row_ref, x_row_ref, x_ref, g_ref, sems):
    frames, rows, cols, chan_in = x_ref.shape
    row = jnp.where(place[1] == 0, rows - 1, 0)
    copies = [pltpu.make_async_copy(x_hbm.at[t], x_ref.at[t], sems.at[t]) for t in range(frames)]
    copies += [pltpu.make_async_copy(g_hbm.at[t], g_ref.at[t], sems.at[frames + t]) for t in range(frames)]
    for copy in copies:
        copy.start()
    firsts, squares = [], []
    for t in range(frames):
        copies[t].wait()
        v = x_ref[t].reshape(rows * cols, chan_in).astype(F32)
        firsts.append(jnp.sum(v, axis=0, keepdims=True))
        squares.append(jnp.sum(v * v, axis=0, keepdims=True))
        x_row_ref[t] = x_ref[t, row]
    total = group_sum(jnp.concatenate(firsts + squares, axis=0), per_group)
    sums_ref[...] = total
    parts = []
    for _ in range(3):
        parts.append(total.astype(BF16).astype(F32))
        total = total - parts[-1]
    n = rows * cols
    odd_ref[2 * n :, :chan_in] = jnp.concatenate(parts[:2], axis=0).astype(BF16)
    odd_ref[2 * n :, chan_in:] = jnp.concatenate([parts[2], jnp.zeros_like(total)], axis=0).astype(BF16)
    for t in range(frames):
        copies[frames + t].wait()
        row_ref[t] = g_ref[t, row]
    even = jnp.bitwise_and(place[0], 1) == 0
    for t in range(2):
        clip, low = x_ref[frames - 2 + t], g_ref[t, :, :, :chan_in]
        here = slice(t * n, (t + 1) * n)
        odd_ref[here, :chan_in] = jnp.where(even, clip, low).reshape(n, chan_in)
        even_ref[t, :, :, :chan_in] = jnp.where(even, low, clip)
        odd_ref[here, chan_in:] = g_ref[t, :, :, chan_in:].reshape(n, chan_in)
        even_ref[t, :, :, chan_in:] = g_ref[t, :, :, chan_in:]


def arrived_kernel(place, odd_ref, even_ref, next_ref, prev_ref, edge_ref):
    chan_in, chan_out = prev_ref.shape[3], next_ref.shape[3]
    even = jnp.bitwise_and(place[0], 1) == 0
    row = jnp.where(place[1] == 0, next_ref.shape[1] - 1, 0)
    n = next_ref.shape[1] * next_ref.shape[2]
    for t in range(2):
        odd = odd_ref[t * n : (t + 1) * n].reshape(next_ref.shape[1:])
        next_ref[t] = jnp.where(even, odd, even_ref[t])
        prev_ref[t] = jnp.where(even, even_ref[t, :, :, :chan_in], odd[:, :, :chan_in])
        edge_ref[t, :, :chan_out] = next_ref[t, row]
        edge_ref[t, :, chan_out:] = prev_ref[t, row]


def frame_stats(place, stats_ref, frames, per_frame):
    devices = stats_ref.shape[0] - 1
    mine = place[0]
    own = stats_ref[0]
    before = jnp.zeros_like(own)
    behind = jnp.zeros_like(own)
    for x in range(1, devices):
        other = jnp.bitwise_xor(mine, x)
        rows = stats_ref[x]
        before = before + jnp.where(other < mine - 1, rows, 0.0)
        behind = behind + jnp.where(other == mine - 1, rows, 0.0)

    def total(rows, at):
        return jnp.sum(rows[at : at + frames], axis=0, keepdims=True)

    first, square = total(before, 0), total(before, frames)
    means, inverses = [], []
    for k in range(2 * frames):
        rows, t = (behind, k) if k < frames else (own, k - frames)
        first = first + rows[t : t + 1]
        square = square + rows[frames + t : frames + t + 1]
        if k < frames - 2:
            continue
        shown = jnp.maximum(mine * frames + k - frames + 1, 1).astype(F32) * per_frame
        mean = first / shown
        variance = square / shown - mean * mean
        means.append(mean)
        inverses.append(lax.rsqrt(variance + 1e-05))
    return means, inverses


def pad_rows(core, own, edge, dst):
    rows = own.shape[1]
    zero = jnp.zeros_like(edge)
    dst[:, 0] = jnp.where(core == 0, zero, edge)
    dst[:, rows + 1] = jnp.where(core == 0, edge, zero)
    dst[:, 1 : rows + 1] = own


def by_taps(window, w_ref, tap, chan_in):
    size = 3 * chan_in
    start = tap * size if isinstance(tap, int) else pl.multiple_of(tap * size, size)
    return lax.dot_general(
        window, w_ref[pl.ds(start, size)], (((1,), (1,)), ((), ())), preferred_element_type=F32
    )


def own_grad_kernel(g_ref, w_ref, z_ref, gp_ref):
    frames, rows, cols, chan_out = g_ref.shape
    chan_in = z_ref.shape[3] // 3
    zero = jnp.zeros((frames, cols, chan_out), BF16)
    gp_ref[:, 0] = zero
    gp_ref[:, rows + 1] = zero
    gp_ref[:, 1 : rows + 1] = g_ref[...]
    for a in (2, 1, 0):
        n = frames - 2 + a
        for b in range(3):
            window = gp_ref[2 - a :, 2 - b : 2 - b + rows].reshape(n * rows * cols, chan_out)
            part = by_taps(window, w_ref, a * 3 + b, chan_in).reshape(n, rows, cols, 3 * chan_in)
            if a == 2 and b == 0:
                z_ref[...] = part
            else:
                z_ref[:n] += part


def gain_kernel(
    per_frame, place, stats_ref, x_ref, own_ref, next_ref, edge_ref, edge_next, w_ref, o_ref, gp_ref, z_ref
):
    frames, rows, cols, chan_out = own_ref.shape[:3] + (next_ref.shape[3],)
    chan_in = x_ref.shape[2]
    cells = rows * cols
    core = place[1]
    pad_rows(core, next_ref[...], edge_next[:, :, :chan_out], gp_ref)
    z_ref[...] = own_ref[...]
    for a in range(2):
        n = 2 - a
        for b in range(3):
            window = gp_ref[:n, 2 - b : 2 - b + rows].reshape(n * cells, chan_out)
            part = by_taps(window, w_ref, a * 3 + b, chan_in).reshape(n, rows, cols, 3 * chan_in)
            z_ref[frames - n :] += part
    row = jnp.where(core == 0, rows - 1, 0)
    tap_row = jnp.where(core == 0, 0, 2)
    for a in range(3):
        n = frames - 2 + a
        window = edge_ref[2 - a : frames].reshape(n * cols, chan_out)
        part = by_taps(window, w_ref, a * 3 + tap_row, chan_in)
        for t in range(n):
            z_ref[t, row] += part[t * cols : (t + 1) * cols]
    means, inverses = frame_stats(place, stats_ref, frames, per_frame)
    affine = stats_ref[stats_ref.shape[0] - 1]
    gain, bias = affine[:1], affine[1:2]
    col = lax.broadcasted_iota(jnp.int32, (cells, chan_in), 0) % cols
    by_gain = jnp.zeros((1, chan_in), F32)
    by_bias = jnp.zeros((1, chan_in), F32)
    for t in range(frames):
        z = z_ref[t].reshape(cells, 3 * chan_in)
        left = jnp.where(col == cols - 1, 0.0, pltpu.roll(z[:, :chan_in], cells - 1, 0))
        right = jnp.where(col == 0, 0.0, pltpu.roll(z[:, 2 * chan_in :], 1, 0))
        grad_hidden = left + z[:, chan_in : 2 * chan_in] + right
        normed = (x_ref[t].astype(F32) - means[2 + t]) * inverses[2 + t]
        act = normed * gain + bias
        sigma = lax.logistic(act)
        grad_act = grad_hidden * sigma * (1.0 + act * (1.0 - sigma))
        by_gain = by_gain + jnp.sum(grad_act * normed, axis=0, keepdims=True)
        by_bias = by_bias + jnp.sum(grad_act, axis=0, keepdims=True)
    o_ref[...] = jnp.concatenate([by_gain, by_bias], axis=0)


def kernel_grad_kernel(
    per_frame, late, skip, place, stats_ref, next_ref, edge_ref, edge_next, x_ref, g_ref, *rest
):
    keep_ref, send_ref, ht_ref, gp_ref = rest
    frames, cells, chan_in = x_ref.shape
    rows, cols, chan_out = g_ref.shape[1:]
    core = place[1]
    pad_rows(core, g_ref[...], edge_ref[...], gp_ref.at[:frames])
    pad_rows(core, next_ref[...], edge_next[:, :, :chan_out], gp_ref.at[frames:])
    means, inverses = frame_stats(place, stats_ref, frames, per_frame)
    affine = stats_ref[stats_ref.shape[0] - 1]
    gain, bias = affine[:1], affine[1:2]
    block = 2 * cols
    lane = lax.broadcasted_iota(jnp.int32, (chan_in, block), 1) % cols
    for t in range(frames):
        for half in range(cells // block):
            v = x_ref[t, half * block : (half + 1) * block].astype(F32)
            act = (v - means[2 + t]) * inverses[2 + t] * gain + bias
            hidden = (act * lax.logistic(act)).astype(BF16).astype(F32)
            turned = hidden.T
            at = t * cells + half * block
            earlier = jnp.where(lane == 0, 0.0, pltpu.roll(turned, 1, 1))
            later = jnp.where(lane == cols - 1, 0.0, pltpu.roll(turned, block - 1, 1))
            for d, piece in enumerate((earlier, turned, later)):
                piece = piece.astype(BF16)
                for k in range(chan_in // 16):
                    to = late(d * (chan_in // 16) + k) * 16
                    ht_ref[to : to + 16, at : at + block] = piece[k * 16 : (k + 1) * 16]
    mine = chan_out // 2
    n = 3 * chan_in
    for a in range(3):
        for b in range(3):
            tap = a * 3 + b
            window = gp_ref[2 - a : 2 - a + frames, 2 - b : 2 - b + rows].reshape(frames * cells, chan_out)
            part = jnp.dot(ht_ref[...], window, preferred_element_type=F32)
            low, high = part[:, :mine], part[:, mine:]
            keep = jnp.where(core == 0, low, high)
            send = jnp.where(core == 0, high, low).astype(BF16)
            for begin, end, at in ((0, skip, tap * skip), (skip, n, 9 * skip + tap * (n - skip))):
                if end > begin:
                    keep_ref[at : at + end - begin] = keep[begin:end]
                    send_ref[at : at + end - begin] = send[begin:end]


def hidden_kernel(
    per_frame, place, stats_ref, x_ref, prev_ref, edge_ref, prev_edge, h_ref
):
    frames, rows, cols, chan_in = x_ref.shape
    mine, core = place[0], place[1]
    means, inverses = frame_stats(place, stats_ref, frames, per_frame)
    affine = stats_ref[stats_ref.shape[0] - 1]
    gain, bias = affine[:1], affine[1:2]

    def put(f, r0, rows_now, value, keep):
        act = (value.astype(F32) - means[f]) * inverses[f] * gain + bias
        hidden = act * lax.logistic(act)
        if keep is not None:
            hidden = jnp.where(keep, hidden, 0.0)
        n = rows_now * cols
        col = lax.broadcasted_iota(jnp.int32, (n, chan_in), 0) % cols
        earlier = jnp.where(col == 0, 0.0, pltpu.roll(hidden, 1, 0))
        later = jnp.where(col == cols - 1, 0.0, pltpu.roll(hidden, n - 1, 0))
        for d, piece in enumerate((earlier, hidden, later)):
            h_ref[f, r0 : r0 + rows_now, :, d * chan_in : (d + 1) * chan_in] = piece.astype(BF16).reshape(
                rows_now, cols, chan_in
            )

    for f in range(frames + 2):
        inside = (mine > 0) if f < 2 else None
        value = prev_ref[f] if f < 2 else x_ref[f - 2]
        put(f, 1, rows, value.reshape(rows * cols, chan_in), inside)
        for r0, here in ((0, core == 1), (rows + 1, core == 0)):
            put(f, r0, 1, prev_edge[f, :, prev_edge.shape[2] - chan_in :] if f < 2 else edge_ref[f - 2], here if inside is None else jnp.logical_and(here, inside))


def output_kernel(h_ref, w_ref, o_ref, acc_ref):
    frames, rows, cols, size = h_ref.shape
    frames, rows = frames - 2, rows - 2
    cells = frames * rows * cols
    for a in range(3):
        for b in range(3):
            tap = a * 3 + b
            window = h_ref[a : a + frames, b : b + rows].reshape(cells, size)
            part = jnp.dot(window, w_ref[tap * size : (tap + 1) * size], preferred_element_type=F32)
            if tap == 0:
                acc_ref[...] = part
            elif tap < 8:
                acc_ref[...] += part
            else:
                o_ref[...] = (acc_ref[...] + part).astype(BF16)


def split_kernel(cut, rest, place, keep_ref, recv_ref, stay1, send1, stay2, *send2):
    tm = len(send2) + 1

    def total(at):
        rows = pl.ds(pl.multiple_of(at, 16), size)
        return keep_ref[rows] + recv_ref[rows].astype(F32)

    size = rest
    stay2[...] = total(place[0] * rest)
    for k, send in zip(OTHERS, send2):
        send[...] = total(jnp.bitwise_xor(place[0], k) * rest).astype(BF16)
    size = cut
    for t in range(tm):
        at = tm * rest + 2 * t * cut
        stay1[t * cut : (t + 1) * cut] = total(at + place[2] * cut)
        send1[t * cut : (t + 1) * cut] = total(at + (1 - place[2]) * cut).astype(BF16)


def put_rider(rider, dst, at):
    parts = []
    for _ in range(3):
        part = rider.astype(BF16)
        rider = rider - part.astype(F32)
        parts.append(part.astype(F32))
    parts.append(jnp.zeros((8 - 3 * rider.shape[0], rider.shape[1]), F32))
    dst[at : at + 8] = jnp.concatenate(parts, axis=0).astype(BF16)


def get_rider(src, at, n):
    rows = src[at : at + 8].astype(F32)
    return (rows[:n] + rows[n : 2 * n]) + rows[2 * n : 3 * n]


def middle_kernel(place, stay1_ref, recv1_ref, stay2_ref, b_ref, c_ref, a_ref, rider_ref, got_ref, *outs):
    stay1, sends, stay2, send2, rider_out = outs[0], outs[1:4], outs[4], outs[5], outs[6]
    rider = rider_ref[...] + got_ref[...]
    rider_out[...] = rider
    n = stay1.shape[0]

    def total(other):
        rows = pl.ds(pl.multiple_of(jnp.bitwise_xor(place[0], other) * n, 16), n)
        return stay1_ref[rows] + recv1_ref[rows].astype(F32)

    stay1[...] = total(0)
    for k, send in zip(OTHERS, sends):
        send[:n] = total(k).astype(BF16)
        put_rider(rider, send, n)
    m = stay2.shape[0]

    def summed(bit):
        rows = pl.ds(pl.multiple_of(bit * m, 16), m)
        first = stay2_ref[rows] + a_ref[rows].astype(F32)
        return first + (b_ref[rows].astype(F32) + c_ref[rows].astype(F32))

    stay2[...] = summed(place[2])
    send2[...] = summed(1 - place[2]).astype(BF16)


def last_kernel(stay1_ref, b_ref, c_ref, a_ref, stay2_ref, recv2_ref, rider_ref, o_ref, gain_ref, bias_ref):
    for k in range(stay2_ref.shape[0] // 16):
        two, one = slice(16 * k, 16 * k + 16), slice(32 * k, 32 * k + 32)
        near = stay1_ref[one] + a_ref[one].astype(F32)
        o_ref[48 * k : 48 * k + 32] = near + (b_ref[one].astype(F32) + c_ref[one].astype(F32))
        o_ref[48 * k + 32 : 48 * k + 48] = stay2_ref[two] + recv2_ref[two].astype(F32)
    n = stay1_ref.shape[0]
    near, b, c = (get_rider(ref, n, 2) for ref in (a_ref, b_ref, c_ref))
    rider = (rider_ref[...] + near) + (b + c)
    gain_ref[...] = rider[:1]
    bias_ref[...] = rider[1:]


def bits_of(axis):
    return [1 << k for k in range((lax.axis_size(axis) - 1).bit_length())]


def swap(value, axis, step):
    return lax.ppermute(value, axis, [(i, i ^ step) for i in range(lax.axis_size(axis))])


def together(*values):
    return lax.optimization_barrier(values)


def all_sum(value, axes):
    for axis in axes:
        for step in bits_of(axis):
            value = value + swap(value, axis, step)
    return value


def parted(value, axis, step):
    value = value.reshape((value.shape[0] // 2, 2) + value.shape[1:])
    bit = jnp.minimum(jnp.bitwise_and(lax.axis_index(axis), step), 1)
    keep = lax.dynamic_index_in_dim(value, bit, 1, keepdims=False)
    send = lax.dynamic_index_in_dim(value, 1 - bit, 1, keepdims=False)
    return keep, send.astype(BF16)


def body(clips, gain, bias, weight, cotangent):
    x, g = clips[0], cotangent[0]
    frames, rows, cols, chan_in = x.shape
    chan_out = g.shape[-1]
    per_group = chan_in // GROUPS
    tm, dp, width = (lax.axis_size(name) for name in ("tm", "dp", "width"))
    per_frame = float(rows * width * cols * per_group)
    z, core = lax.axis_index("tm"), lax.axis_index("width")
    place = jnp.stack([z, core, lax.axis_index("dp")]).astype(jnp.int32)
    cells = rows * cols
    shape = jax.ShapeDtypeStruct
    half = chan_out // 2

    odd_pairs = [(i, i ^ 1) for i in range(tm)]
    even_pairs = [(i, i + 1 if i % 2 else i - 1) for i in range(1, tm - 1)]
    affine = jnp.pad(jnp.stack([gain, bias]), ((0, 2 * frames - 2), (0, 0)))[None]
    x, g, place = together(x, g, place)
    sums, to_odd, to_even, g_rows, x_rows, x_near, g_near = call(
        functools.partial(prepare_kernel, per_group),
        (
            shape((2 * frames, chan_in), F32),
            shape((2 * cells + 4 * frames, chan_out), BF16),
            shape((2, rows, cols, chan_out), BF16),
            shape((frames, cols, chan_out), BF16),
            shape((frames, cols, chan_in), BF16),
            shape(x.shape, BF16),
            shape(g.shape, BF16),
        ),
        [place, far(x), far(g)],
        [pltpu.SemaphoreType.DMA((2 * frames,))],
        scalars=1,
        far=2,
    )
    from_odd = lax.ppermute(to_odd, "tm", odd_pairs)
    from_even = lax.ppermute(to_even, "tm", even_pairs)
    g_edge = swap(g_rows, "width", 1)
    x_edge = swap(x_rows, "width", 1)
    x, g = x_near, g_near
    flat = x.reshape(frames, cells, chan_in)
    sums, g = together(sums, g)
    own_grad = call(
        own_grad_kernel,
        shape((frames, rows, cols, 3 * chan_in), F32),
        [g, weight],
        [pltpu.VMEM((frames, rows + 2, cols, chan_out), BF16)],
    )
    sums, from_odd, g_edge, x_edge, own_grad = together(sums, from_odd, g_edge, x_edge, own_grad)

    g_next, x_prev, next_edge = call(
        arrived_kernel,
        (
            shape((2, rows, cols, chan_out), BF16),
            shape((2, rows, cols, chan_in), BF16),
            shape((2, cols, chan_out + chan_in), BF16),
        ),
        [place, from_odd, from_even],
        scalars=1,
    )
    next_edge = swap(next_edge, "width", 1)
    near = from_odd[2 * cells :].astype(F32)
    near = (near[: 2 * frames, :chan_in] + near[2 * frames :, :chan_in]) + near[: 2 * frames, chan_in:]
    stats = jnp.stack([sums, near])
    for step in bits_of("tm")[1:]:
        stats = jnp.concatenate([stats, swap(stats, "tm", step)], axis=0)
    stats, next_edge, g_next, x_prev = together(stats, next_edge, g_next, x_prev)
    stats = stats + swap(stats, "width", 1)
    stats = jnp.concatenate([stats, affine], axis=0)

    share = 27 * chan_in // (tm * dp)
    pieces = share % 48 == 0 and tm == 4 and dp == 2
    count = 3 * chan_in // 48
    if pieces:
        skip = chan_in
        late = lambda k: k // 3 if k % 3 == 2 else count + k // 3 * 2 + k % 3
    else:
        skip = 0
        late = lambda k: k
    keep, send = call(
        functools.partial(kernel_grad_kernel, per_frame, late, skip),
        (shape((27 * chan_in, half), F32), shape((27 * chan_in, half), BF16)),
        [place, stats, g_next, g_edge, next_edge, flat, g],
        [
            pltpu.VMEM((3 * chan_in, frames * cells), BF16),
            pltpu.VMEM((frames + 2, rows + 2, cols, chan_out), BF16),
        ],
        scalars=1,
    )
    send, hold = together(send, stats)
    recv = swap(send, "width", 1)
    local = call(
        functools.partial(gain_kernel, per_frame),
        shape((2, chan_in), F32),
        [place, hold, flat, own_grad, g_next, g_edge, next_edge, weight],
        [
            pltpu.VMEM((2, rows + 2, cols, chan_out), BF16),
            pltpu.VMEM((frames, rows, cols, 3 * chan_in), F32),
        ],
        scalars=1,
    )
    recv, local = together(recv, local)

    def activations(hold):
        return call(
            functools.partial(hidden_kernel, per_frame),
            shape((frames + 2, rows + 2, cols, 3 * chan_in), BF16),
            [place, hold, x, x_prev, x_edge, next_edge],
            scalars=1,
        )

    def outputs(hidden):
        return call(
            output_kernel,
            shape((frames * cells, chan_out), BF16),
            [hidden, weight],
            [pltpu.VMEM((frames * cells, chan_out), F32)],
        )

    if not pieces:
        output = outputs(activations(stats))
        one = keep + recv.astype(F32)
        one = jnp.moveaxis(one.reshape(tm, dp, share, half), 1, 0)
        for step in bits_of("dp"):
            one, send = parted(one, "dp", step)
            one = one + swap(send, "dp", step).astype(F32)
        one = one[0]
        for step in bits_of("tm"):
            one, send = parted(one, "tm", step)
            one = one + swap(send, "tm", step).astype(F32)
        rider = all_sum(local, ("width", "dp", "tm"))
        grad_weight = one[0]
    else:
        rest = share // 3
        cut = share - rest

        def piece(n, kind):
            return shape((n, half), kind)

        both = dp * rest
        stay1, send1, stay2, *send2 = call(
            functools.partial(split_kernel, cut, both),
            [piece(tm * cut, F32), piece(tm * cut, BF16), piece(both, F32)] + [piece(both, BF16)] * (tm - 1),
            [place, keep, recv],
            scalars=1,
        )
        rider = local + swap(local, "width", 1)
        send1, hold, rider, *send2 = together(send1, hold, rider, *send2)
        recv2 = [swap(send2[0], "tm", OTHERS[0])]
        recv1 = swap(send1, "dp", 1)
        recv2 += [swap(v, "tm", k) for k, v in zip(OTHERS[1:], send2[1:])]
        got = swap(rider, "dp", 1)
        recv1, got, hidden, *recv2 = together(recv1, got, activations(hold), *recv2)
        stay1, *send1, stay2, send2, rider = call(
            middle_kernel,
            [piece(cut, F32)]
            + [piece(cut + 8, BF16)] * (tm - 1)
            + [piece(rest, F32), piece(rest, BF16), shape(rider.shape, F32)],
            [place, stay1, recv1, stay2, *recv2, rider, got],
            scalars=1,
        )
        send2, hidden, *send1 = together(send2, hidden, *send1)
        recv1 = [swap(v, "tm", k) for k, v in zip(OTHERS, send1)]
        recv2 = swap(send2, "dp", 1)
        output = outputs(hidden)
        recv2, output, *recv1 = together(recv2, output, *recv1)
        row = shape((1, chan_in), F32)
        grad_weight, *rider = call(
            last_kernel, [piece(share, F32), row, row], [stay1, *recv1, stay2, recv2, rider]
        )
        rider = [v.reshape(chan_in) for v in rider]
    return (output.reshape(1, frames, rows, cols, chan_out), grad_weight, rider[0], rider[1])


def solution(mesh):
    return jax.shard_map(
        body,
        mesh=mesh,
        in_specs=(
            P(("groups", "dp"), "tm", "width", None, None),
            P(),
            P(),
            P(),
            P(("groups", "dp"), "tm", "width", None, None),
        ),
        out_specs=(
            P(("groups", "dp"), "tm", "width", None, None),
            P(("groups", "tm", "dp"), "width"),
            P("groups"),
            P("groups"),
        ),
        check_vma=False,
    )
```
